256 devices in a mesh: dp: 32 (over y, x, core), ctx: 8 (over z).
Axes of the slice: x: 4, y: 4, z: 8, core: 2. Of those that a mesh axis runs over, the one named last changes fastest.
Arguments:
- value: bfloat16 [32, 1024, 512], P('dp', 'ctx'), may hold values from -6 to 6
- gate_one: bfloat16 [32, 1024, 512], P('dp', 'ctx'), may hold values from -6 to 6
- gate_two: bfloat16 [32, 1024, 512], P('dp', 'ctx'), may hold values from -6 to 6
- filters: bfloat16 [2, 1024, 512], replicated, may hold values from -0.1875 to 0.1875
- out_weight: bfloat16 [512, 512], replicated, may hold values from -0.25 to 0.25
- grad_out: bfloat16 [32, 1024, 512], P('dp', 'ctx'), may hold values from -6 to 6
Outputs:
- mixed: bfloat16 [32, 1024, 512], P('dp', 'ctx')
- grad_value: bfloat16 [32, 1024, 512], P('dp', 'ctx')
- grad_gate_one: bfloat16 [32, 1024, 512], P('dp', 'ctx')
- grad_gate_two: bfloat16 [32, 1024, 512], P('dp', 'ctx')
- filter_grad: float32 [2, 1024, 512], P(None, 'ctx', 'dp')
- weight_grad: float32 [512, 512], P('dp', 'ctx')
The draws below stay inside these ranges and needn't reach their ends.
All inputs are finite; a program needn't handle non-finite values.
Results may differ from the reference program's by a relative error of at most 0.019.
Values may be sent and summed in bfloat16 or wider, within the bound.
A program may use at most 128 MiB of HBM per device.

```python
import jax
import jax.numpy as jnp

D = 512
LENGTH = 1024
DOCS = 32


def levels(stream_key, shape, pieces, smallest, high):
    loudness = 1.0
    for dim, parts in pieces:
        steps = jax.random.uniform(jax.random.fold_in(jax.random.fold_in(stream_key, 6), dim), (parts,), jnp.float32, smallest / len(pieces), high / len(pieces))
        loudness = loudness * jnp.repeat(jnp.exp(steps), shape[dim] // parts).reshape((-1,) + (1,) * (len(shape) - 1 - dim))
    return loudness


def bell_draw(own_key, dims, scale, most, pieces=(), held_as=jnp.bfloat16):
    array = jax.random.normal(own_key, dims, jnp.float32) * scale
    if len(pieces) > 0:
        array = levels(own_key, dims, pieces, -0.22, 0.18) * array
    return jnp.clip(array, min=-most, max=most).astype(held_as)


def setup_inputs(seed: int = 0) -> dict:
    seeds = jax.random.split(jax.random.key(seed), 7)
    value = bell_draw(seeds[0], (DOCS, LENGTH, D), 1.0, 6.0, ((0, 32), (1, 8)))
    gate_one = bell_draw(seeds[1], (DOCS, LENGTH, D), 1.0, 6.0, ((0, 32), (1, 8)))
    gate_two = bell_draw(seeds[2], (DOCS, LENGTH, D), 1.0, 6.0, ((0, 32), (1, 8)))
    filters = bell_draw(seeds[3], (2, LENGTH, D), LENGTH ** -0.5, 0.1875)
    out_weight = bell_draw(seeds[4], (D, D), D ** -0.5, 0.25)
    grad_out = bell_draw(seeds[5], (DOCS, LENGTH, D), 1.0, 6.0, ((0, 32), (1, 8)))
    return dict(value=value, gate_one=gate_one, gate_two=gate_two, filters=filters, out_weight=out_weight, grad_out=grad_out)


def causal(filt, stream):
    length = stream.shape[1]
    width = 2 * length
    filter_freq = jnp.fft.rfft(filt.astype(jnp.float32), n=width, axis=0)
    stream_freq = jnp.fft.rfft(stream.astype(jnp.float32), n=width, axis=1)
    return jnp.fft.irfft(filter_freq[None] * stream_freq, n=width, axis=1)[:, :length]


def anti_causal(filt, grads):
    return jnp.flip(causal(filt, jnp.flip(grads, 1)), 1)


def filter_terms(stream, grads):
    length = stream.shape[1]
    width = 2 * length
    stream_freq = jnp.fft.rfft(stream.astype(jnp.float32), n=width, axis=1)
    grad_freq = jnp.fft.rfft(grads.astype(jnp.float32), n=width, axis=1)
    summed = jnp.sum(jnp.conj(stream_freq) * grad_freq, axis=0)
    return jnp.fft.irfft(summed, n=width, axis=0)[:length]


def reference(value, gate_one, gate_two, filters, out_weight, grad_out):
    first_conv = causal(filters[0], value)
    mixed_input = (gate_one.astype(jnp.float32) * first_conv).astype(jnp.bfloat16)
    second_conv = causal(filters[1], mixed_input)
    gated = (gate_two.astype(jnp.float32) * second_conv).astype(jnp.bfloat16)
    flat_gated = gated.reshape(-1, D)
    flat_grad = grad_out.reshape(-1, D)
    mixed = jnp.dot(flat_gated, out_weight, preferred_element_type=jnp.float32).astype(jnp.bfloat16).reshape(value.shape)
    grad_gated = jnp.dot(flat_grad, out_weight.T, preferred_element_type=jnp.float32).reshape(value.shape)
    grad_gate_two = (grad_gated * second_conv).astype(jnp.bfloat16)
    grad_second = (grad_gated * gate_two.astype(jnp.float32)).astype(jnp.bfloat16)
    grad_mixed = anti_causal(filters[1], grad_second)
    grad_gate_one = (grad_mixed * first_conv).astype(jnp.bfloat16)
    grad_first = (grad_mixed * gate_one.astype(jnp.float32)).astype(jnp.bfloat16)
    grad_value = anti_causal(filters[0], grad_first).astype(jnp.bfloat16)
    filter_grad = jnp.stack([filter_terms(value, grad_first), filter_terms(mixed_input, grad_second)]) / DOCS
    weight_grad = jnp.dot(flat_gated.T, flat_grad, preferred_element_type=jnp.float32) / DOCS
    return mixed, grad_value, grad_gate_one, grad_gate_two, filter_grad, weight_grad
```

```python
import numpy as np

import jax
import jax.numpy as jnp
from jax import lax
from jax.experimental import pallas as pl
from jax.experimental.pallas import tpu as pltpu
from jax.sharding import PartitionSpec as P

F32 = jnp.float32
BF16 = jnp.bfloat16
MESH = pl.DeviceIdType.MESH

CTX = 8
CHIPS = 16
WIDTH = 512
ROWS = 128
BLK = 256
BINS = 256
CHUNK = 16


def tables():
    bins = np.concatenate([np.arange(0, BINS, 2), np.arange(1, BINS, 2)])
    angle = 2.0 * np.pi * (bins[:, None] + 0.5) * np.arange(BLK)[None, :] / (2 * BLK)
    forward = np.concatenate([np.cos(angle), -np.sin(angle)], axis=0)
    inverse = forward.T / BINS

    def split(table):
        high = table.astype(BF16)
        low = (table - high.astype(np.float64)).astype(BF16)
        return high, low

    return split(forward) + split(inverse)


def lanes_low(rows):
    return lax.broadcasted_iota(jnp.int32, (rows, 128), 1) < 64


def turn(x, shift=64):
    return pltpu.roll(x, shift, 1)


def mix(a, b):
    low = lanes_low(a.shape[0])
    return jnp.where(low, a, turn(b)), jnp.where(low, turn(a), b)


def kernel(
    value, gate_one, gate_two, grad_out, filters, weight, fh, fl, ih, il,
    mixed, grad_value, grad_gate_one, grad_gate_two, filter_grad, weight_grad,
    sbuf, rbuf, filt, g_first, g_second, v_spec, m_spec, s_spec, f_spec, p_high, p_low,
    first_conv, grad_gated, xt,
    w_part, w_pair, w_sum, w_plane, w_tiles, w_ring,
    f_part, f_pair, f_sum, f_plane, f_send, f_recv,
    filt_sem, z_send, z_recv, pair_send, pair_recv, plane_send, plane_recv,
    ring_send, ring_recv, swap_send, swap_recv,
):
    doc = lax.axis_index("dp")
    pos = lax.axis_index("ctx")
    core = lax.rem(doc, 2)
    chip = lax.div(doc, 2)
    swap_doc = 4 * pos + lax.rem(doc, 4)
    swap_pos = lax.div(doc, 4)
    swap_self = swap_pos == pos

    column = pl.multiple_of(lax.div(pos, 2) * 128, 128)
    filt_copy = pltpu.make_async_copy(filters.at[:, :, pl.ds(column, 128)], filt, filt_sem)
    filt_copy.start()

    barrier = pltpu.get_barrier_semaphore()
    for o in range(1, CTX):
        pl.semaphore_signal(barrier, inc=1, device_id=(doc, lax.rem(pos + o, CTX)), device_id_type=MESH)
    pl.semaphore_signal(barrier, inc=1, device_id=(2 * chip + 1 - core, pos), device_id_type=MESH)
    for o in range(1, CHIPS):
        peer = 2 * lax.rem(chip + o, CHIPS) + core
        pl.semaphore_signal(barrier, inc=1, device_id=(peer, pos), device_id_type=MESH)

    @pl.when(jnp.logical_not(swap_self))
    def _():
        pl.semaphore_signal(barrier, inc=1, device_id=(swap_doc, swap_pos), device_id_type=MESH)

    def pack_rows(slot, tile_of):
        for p in range(4):
            first, second = mix(tile_of(0, p), tile_of(1, p))
            sbuf[slot, 2 * p] = first.astype(BF16)
            sbuf[slot, 2 * p + 1] = second.astype(BF16)
        rbuf[slot, pos] = sbuf[slot, pos]

    def pack_blocks(slot, tiles):
        for t in range(2):
            for h in range(2):
                part = tiles[t][128 * h : 128 * h + 128]
                first, second = mix(part[:64], part[64:])
                sbuf[slot, 4 * t + h] = first.astype(BF16)
                sbuf[slot, 4 * t + 2 + h] = second.astype(BF16)
        rbuf[slot, pos] = sbuf[slot, pos]

    def ring_copy(slot, to, at):
        return pltpu.make_async_remote_copy(
            src_ref=sbuf.at[slot, to],
            dst_ref=rbuf.at[slot, at],
            send_sem=z_send.at[slot, to],
            recv_sem=z_recv.at[slot, at],
            device_id=(doc, to),
            device_id_type=MESH,
        )

    def ring_start(slot):
        for o in (4, 3, 5, 2, 6, 1, 7):
            ring_copy(slot, lax.rem(pos + o, CTX), pos).start()

    def ring_wait(slot):
        for o in (1, 7, 2, 6, 3, 5, 4):
            src = lax.rem(pos + o, CTX)
            ring_copy(slot, src, src).wait_recv()

    def rows_tile(ref):
        return lambda h, p: ref[64 * h : 64 * h + 64, 128 * p : 128 * p + 128].astype(F32)

    pack_rows(0, rows_tile(value))
    pack_rows(1, rows_tile(gate_one))
    grad_gated[...] = lax.dot_general(
        grad_out[...], weight[...], (((1,), (1,)), ((), ())), preferred_element_type=F32
    )
    pack_rows(
        2,
        lambda h, p: (
            grad_gated[64 * h : 64 * h + 64, 128 * p : 128 * p + 128]
            * gate_two[64 * h : 64 * h + 64, 128 * p : 128 * p + 128].astype(F32)
        ).astype(BF16).astype(F32),
    )
    pl.semaphore_wait(barrier, 23 + jnp.where(swap_self, 0, 1))
    ring_start(0)
    ring_start(1)
    ring_start(2)

    def forward(spec):
        block = xt[...]
        spec[...] = jnp.dot(fh[...], block, preferred_element_type=F32) + jnp.dot(
            fl[...], block, preferred_element_type=F32
        )

    def inverse():
        high = p_high[...]
        return (
            jnp.dot(ih[...], high, preferred_element_type=F32)
            + jnp.dot(il[...], high, preferred_element_type=F32)
            + jnp.dot(ih[...], p_low[...], preferred_element_type=F32)
        )

    def load(spec, r):
        a = spec[pl.ds(r, CHUNK), :]
        b = spec[pl.ds(BINS + r, CHUNK), :]
        return (a[:, :128], b[:, :128]), (a[:, 128:], b[:, 128:])

    def store(r, low_blocks, high_blocks):
        for part in range(2):
            for t, block in enumerate((low_blocks, high_blocks)):
                x = block[part]
                high = x.astype(BF16)
                where = (pl.ds(part * BINS + r, CHUNK), slice(128 * t, 128 * t + 128))
                p_high[where] = high
                p_low[where] = (x - high.astype(F32)).astype(BF16)

    def both(x):
        return tuple(turn(part) for part in x)

    def pick(a, b):
        low = lanes_low(CHUNK)
        return tuple(jnp.where(low, x, y) for x, y in zip(a, b))

    def low_only(x):
        return pick(x, (jnp.zeros_like(x[0]),) * 2)

    def high_only(x):
        return pick((jnp.zeros_like(x[0]),) * 2, x)

    def times(a, b):
        return a[0] * b[0] - a[1] * b[1], a[0] * b[1] + a[1] * b[0]

    def conj_times(a, b):
        return a[0] * b[0] + a[1] * b[1], a[0] * b[1] - a[1] * b[0]

    def plus(*terms):
        return sum(t[0] for t in terms[1:]) + terms[0][0], sum(t[1] for t in terms[1:]) + terms[0][1]

    def chunks(body):
        for half, sign in ((0, 1.0), (1, -1.0)):

            def step(i, carry):
                body(pl.multiple_of(half * (BINS // 2) + i * CHUNK, CHUNK), sign)
                return carry

            lax.fori_loop(0, BINS // 2 // CHUNK, step, 0)

    def spread(g01, g23):
        t01, t23 = both(g01), both(g23)
        return pick(g01, t01), pick(t01, g01), pick(g23, t23), t01, t23

    def convolve(filter_spec, data_spec):
        def body(r, sign):
            g01, g23 = load(filter_spec, r)
            x01, x23 = load(data_spec, r)
            h0, h1, h2, _, _ = spread(g01, g23)
            x10, x32 = both(x01), both(x23)
            x12 = pick(x10, x32)
            out01 = plus(times(h0, x01), times(high_only(g01), x10))
            out23 = plus(times(h0, x23), times(h1, x12), times(h2, x01), times(high_only(g23), x10))
            store(r, out01, out23)

        chunks(body)

    def correlate(filter_spec, data_spec, windows):
        def body(r, sign):
            g01, g23 = load(filter_spec, r)
            y01, y23 = load(data_spec, r)
            if windows:
                t01, t23 = both(y01), both(y23)
                n01, n23 = pick(t01, t23), low_only(t23)
                y01 = (y01[0] + sign * n01[1], y01[1] - sign * n01[0])
                y23 = (y23[0] + sign * n23[1], y23[1] - sign * n23[0])
            h0, h1, h2, t01, t23 = spread(g01, g23)
            y10, y32 = both(y01), both(y23)
            y12 = pick(y10, y32)
            out01 = plus(
                conj_times(h0, y01), conj_times(h1, y12), conj_times(h2, y23), conj_times(low_only(t23), y32)
            )
            out23 = plus(conj_times(h0, y23), conj_times(low_only(t01), y32))
            store(r, out01, out23)

        chunks(body)

    filt_copy.wait()
    odd = lax.rem(pos, 2) == 1
    for which, spec in ((0, g_first), (1, g_second)):
        for t in range(2):
            lag_tiles = []
            for k in (2 * t, 2 * t + 1):
                tile = filt[which, BLK * k : BLK * k + BLK, :].astype(F32)
                lag_tiles.append(jnp.where(odd, turn(tile), tile))
            xt[:, 128 * t : 128 * t + 128] = mix(*lag_tiles)[0].astype(BF16)
        forward(spec)

        def window(r, sign, spec=spec):
            h01, h23 = load(spec, r)
            t01, t23 = both(h01), both(h23)
            b01, b23 = high_only(t01), pick(t01, t23)
            for t, (h, b) in enumerate(((h01, b01), (h23, b23))):
                spec[pl.ds(r, CHUNK), 128 * t : 128 * t + 128] = h[0] - sign * b[1]
                spec[pl.ds(BINS + r, CHUNK), 128 * t : 128 * t + 128] = h[1] + sign * b[0]

        chunks(window)

    def arrived(slot, t, h):
        return mix(rbuf[slot, 4 * t + h].astype(F32), rbuf[slot, 4 * t + 2 + h].astype(F32))

    def to_columns(slot, scale=None):
        for t in range(2):
            for h in range(2):
                for half, part in enumerate(arrived(slot, t, h)):
                    where = (
                        slice(128 * h + 64 * half, 128 * h + 64 * half + 64),
                        slice(128 * t, 128 * t + 128),
                    )
                    if scale is not None:
                        part = part * scale[where]
                    xt[where] = part.astype(BF16)

    def split_tiles(x):
        return x[:, :128], x[:, 128:]

    ring_wait(0)
    to_columns(0)
    forward(v_spec)
    convolve(g_first, v_spec)
    first_conv[...] = inverse()
    ring_wait(1)
    to_columns(1, first_conv)
    forward(m_spec)
    convolve(g_second, m_spec)
    pack_blocks(3, split_tiles(inverse()))
    ring_start(3)

    ring_wait(2)
    to_columns(2)
    forward(s_spec)
    correlate(g_second, s_spec, False)
    grad_mixed = inverse()
    pack_blocks(4, split_tiles(grad_mixed * first_conv[...]))
    ring_start(4)
    first_conv[...] = grad_mixed
    to_columns(1, first_conv)
    forward(f_spec)
    correlate(g_first, f_spec, False)
    pack_blocks(5, split_tiles(inverse()))
    ring_start(5)

    lane_group = lax.div(lax.broadcasted_iota(jnp.int32, (16, 128), 1), 16)
    for which, stream, grads in ((0, v_spec, f_spec), (1, m_spec, s_spec)):
        correlate(stream, grads, True)
        lags = inverse()
        for h in range(2):
            for t in range(2):
                part = lags[128 * h : 128 * h + 128, 128 * t : 128 * t + 128]
                groups = [part[16 * g : 16 * g + 16] for g in range(8)]
                for s in (4, 2, 1):
                    keep = lax.rem(lax.div(lane_group, s), 2) == 0
                    for g in range(8):
                        if g & s == 0:
                            a, b = groups[g], groups[g | s]
                            groups[g] = jnp.where(keep, a, turn(b, 16 * s))
                            groups[g | s] = jnp.where(keep, turn(a, 128 - 16 * s), b)
                for u in range(8):
                    lag_block = 2 * (2 * t + u // 4) + h
                    q = u % 4
                    f_part[q % 2, 2 * lag_block + q // 2, 16 * which : 16 * which + 16, :] = groups[u].astype(BF16)

    def pair_copy(index, src, dst):
        return pltpu.make_async_remote_copy(
            src_ref=src.at[1 - core],
            dst_ref=dst,
            send_sem=pair_send.at[index],
            recv_sem=pair_recv.at[index],
            device_id=(2 * chip + 1 - core, pos),
            device_id_type=MESH,
        )

    def plane_copy(index, src, dst, to, at):
        return pltpu.make_async_remote_copy(
            src_ref=src.at[to],
            dst_ref=dst.at[at],
            send_sem=plane_send.at[index, to],
            recv_sem=plane_recv.at[index, at],
            device_id=(2 * to + core, pos),
            device_id_type=MESH,
        )

    def plane_start(index, src, dst):
        for o in range(1, CHIPS):
            plane_copy(index, src, dst, lax.rem(chip + o, CHIPS), chip).start()

    def plane_wait(index, src, dst):
        for o in range(1, CHIPS):
            at = lax.rem(chip + o, CHIPS)
            plane_copy(index, src, dst, at, at).wait_recv()

    f_pair_copy = pair_copy(0, f_part, f_pair)
    f_pair_copy.start()

    def row_tile(slot, p):
        return mix(rbuf[slot, 2 * p].astype(F32), rbuf[slot, 2 * p + 1].astype(F32))

    ring_wait(3)
    for p in range(4):
        for half, part in enumerate(row_tile(3, p)):
            where = (slice(64 * half, 64 * half + 64), slice(128 * p, 128 * p + 128))
            grad_gate_two[where] = (grad_gated[where] * part).astype(BF16)
            grad_gated[where] = (gate_two[where].astype(F32) * part).astype(BF16).astype(F32)
    gated = grad_gated[...].astype(BF16)
    gated_t = grad_gated[...].T.astype(BF16)
    for c in range(4):
        part = jnp.dot(
            gated_t[128 * c : 128 * c + 128], grad_out[...], preferred_element_type=F32
        ).astype(BF16)
        for i in range(8):
            row = 16 * (4 * c + i // 2)
            w_part[i % 2, 4 * c + i // 2] = part[16 * i : 16 * i + 16]
    w_pair_copy = pair_copy(1, w_part, w_pair)
    w_pair_copy.start()
    mixed[...] = jnp.dot(gated, weight[...], preferred_element_type=F32).astype(BF16)

    f_pair_copy.wait_recv()
    f_sum[...] = (f_part[core].astype(F32) + f_pair[...].astype(F32)).astype(BF16)
    plane_start(0, f_sum, f_plane)
    f_plane[chip] = f_sum[chip]
    w_pair_copy.wait_recv()
    w_sum[...] = (w_part[core].astype(F32) + w_pair[...].astype(F32)).astype(BF16)
    plane_start(1, w_sum, w_plane)
    w_plane[chip] = w_sum[chip]

    for slot, out in ((4, grad_gate_one), (5, grad_value)):
        ring_wait(slot)
        for p in range(4):
            for half, part in enumerate(row_tile(slot, p)):
                out[64 * half : 64 * half + 64, 128 * p : 128 * p + 128] = part.astype(BF16)

    scale = 1.0 / 32

    plane_wait(0, f_sum, f_plane)
    f_send[...] = jnp.sum(f_plane[...].astype(F32), axis=0) * scale
    swap = pltpu.make_async_remote_copy(
        src_ref=f_send,
        dst_ref=f_recv,
        send_sem=swap_send,
        recv_sem=swap_recv,
        device_id=(swap_doc, swap_pos),
        device_id_type=MESH,
    )

    @pl.when(jnp.logical_not(swap_self))
    def _():
        swap.start()

    @pl.when(swap_self)
    def _():
        f_recv[...] = f_send[...]

    def tile_copy(to, at):
        return pltpu.make_async_remote_copy(
            src_ref=w_tiles.at[lax.div(to, 2)],
            dst_ref=w_ring.at[at],
            send_sem=ring_send.at[to],
            recv_sem=ring_recv.at[at],
            device_id=(doc, to),
            device_id_type=MESH,
        )

    plane_wait(1, w_sum, w_plane)
    w_total = jnp.sum(w_plane[...].astype(F32), axis=0).astype(BF16)
    for p in range(4):
        w_tiles[p] = w_total[:, 128 * p : 128 * p + 128]
    for o in (4, 3, 5, 2, 6, 1, 7):
        tile_copy(lax.rem(pos + o, CTX), pos).start()
    w_ring[pos] = w_tiles[lax.div(pos, 2)]
    for o in range(1, CTX):
        src = lax.rem(pos + o, CTX)
        tile_copy(src, src).wait_recv()
    total = jnp.sum(w_ring[...].astype(F32), axis=0) * scale
    weight_grad[...] = jnp.where(odd, turn(total), total)[:, :64]

    @pl.when(jnp.logical_not(swap_self))
    def _():
        swap.wait_recv()

    for which in range(2):
        packed = f_recv[16 * which : 16 * which + 16, :]
        for g in range(8):
            rows = packed if g == 0 else turn(packed, 128 - 16 * g)
            filter_grad[which, 16 * g : 16 * g + 16, :] = rows[:, :16]

    for slot in range(6):
        for o in range(1, CTX):
            ring_copy(slot, lax.rem(pos + o, CTX), pos).wait_send()
    f_pair_copy.wait_send()
    w_pair_copy.wait_send()
    for index, src, dst in ((0, f_sum, f_plane), (1, w_sum, w_plane)):
        for o in range(1, CHIPS):
            plane_copy(index, src, dst, lax.rem(chip + o, CHIPS), chip).wait_send()
    for o in range(1, CTX):
        tile_copy(lax.rem(pos + o, CTX), pos).wait_send()

    @pl.when(jnp.logical_not(swap_self))
    def _():
        swap.wait_send()


def on_device(value, gate_one, gate_two, filters, out_weight, grad_out):
    vmem = pl.BlockSpec(memory_space=pltpu.VMEM)
    stream = jax.ShapeDtypeStruct((ROWS, WIDTH), BF16)
    spectrum = pltpu.VMEM((2 * BINS, 256), F32)
    dma = pltpu.SemaphoreType.DMA
    outs = pl.pallas_call(
        kernel,
        out_shape=(
            stream,
            stream,
            stream,
            stream,
            jax.ShapeDtypeStruct((2, ROWS, 16), F32),
            jax.ShapeDtypeStruct((16, 64), F32),
        ),
        in_specs=[vmem] * 4 + [pl.BlockSpec(memory_space=pl.ANY)] + [vmem] * 5,
        out_specs=[vmem] * 6,
        scratch_shapes=[
            pltpu.VMEM((6, CTX, 64, 128), BF16),
            pltpu.VMEM((6, CTX, 64, 128), BF16),
            pltpu.VMEM((2, 1024, 128), BF16),
            spectrum, spectrum, spectrum, spectrum, spectrum, spectrum,
            pltpu.VMEM((2 * BINS, 256), BF16),
            pltpu.VMEM((2 * BINS, 256), BF16),
            pltpu.VMEM((BLK, 256), F32),
            pltpu.VMEM((ROWS, WIDTH), F32),
            pltpu.VMEM((BLK, 256), BF16),
            pltpu.VMEM((2, CHIPS, 16, WIDTH), BF16),
            pltpu.VMEM((CHIPS, 16, WIDTH), BF16),
            pltpu.VMEM((CHIPS, 16, WIDTH), BF16),
            pltpu.VMEM((CHIPS, 16, WIDTH), BF16),
            pltpu.VMEM((4, 16, 128), BF16),
            pltpu.VMEM((CTX, 16, 128), BF16),
            pltpu.VMEM((2, CHIPS, 32, 128), BF16),
            pltpu.VMEM((CHIPS, 32, 128), BF16),
            pltpu.VMEM((CHIPS, 32, 128), BF16),
            pltpu.VMEM((CHIPS, 32, 128), BF16),
            pltpu.VMEM((32, 128), F32),
            pltpu.VMEM((32, 128), F32),
            dma,
            dma((6, CTX)),
            dma((6, CTX)),
            dma((2,)),
            dma((2,)),
            dma((2, CHIPS)),
            dma((2, CHIPS)),
            dma((CTX,)),
            dma((CTX,)),
            dma,
            dma,
        ],
        compiler_params=pltpu.CompilerParams(collective_id=0, has_side_effects=True),
    )(
        value[0], gate_one[0], gate_two[0], grad_out[0], filters, out_weight,
        *(jnp.asarray(table) for table in tables()),
    )
    mixed, grad_value, grad_gate_one, grad_gate_two, filter_grad, weight_grad = outs
    return mixed[None], grad_value[None], grad_gate_one[None], grad_gate_two[None], filter_grad, weight_grad


def solution(mesh):
    stream = P("dp", "ctx", None)
    return jax.shard_map(
        on_device,
        mesh=mesh,
        in_specs=(stream, stream, stream, P(), P(), stream),
        out_specs=(stream, stream, stream, stream, P(None, "ctx", "dp"), P("dp", "ctx")),
        check_vma=False,
    )
```

```python
import numpy as np

import jax
import jax.numpy as jnp
from jax import lax
from jax.experimental import pallas as pl
from jax.experimental.pallas import tpu as pltpu
from jax.sharding import PartitionSpec as P

F32 = jnp.float32
BF16 = jnp.bfloat16
MESH = pl.DeviceIdType.MESH

CTX = 8
CHIPS = 16
WIDTH = 512
ROWS = 128
BLK = 256
BINS = 256
CHUNK = 16
UNROLL = 8


def tables():
    bins = np.concatenate([np.arange(0, BINS, 2), np.arange(1, BINS, 2)])
    angle = 2.0 * np.pi * (bins[:, None] + 0.5) * np.arange(BLK)[None, :] / (2 * BLK)
    forward = np.concatenate([np.cos(angle), -np.sin(angle)], axis=0)
    inverse = forward.T / BINS

    def split(table):
        high = table.astype(BF16)
        low = (table - high.astype(np.float64)).astype(BF16)
        return high, low

    return split(forward) + split(inverse)[:1]


def lanes_low(rows):
    return lax.broadcasted_iota(jnp.int32, (rows, 128), 1) < 64


def turn(x, shift=64):
    return pltpu.roll(x, shift, 1)


def mix(a, b):
    low = lanes_low(a.shape[0])
    return jnp.where(low, a, turn(b)), jnp.where(low, turn(a), b)


def kernel(
    value_hbm, gate_one_hbm, gate_two_hbm, grad_out_hbm, filters_hbm, weight_hbm, fh_hbm, fl_hbm, ih_hbm,
    mixed, grad_value, grad_gate_one, grad_gate_two, filter_grad, weight_grad,
    value, gate_one, gate_two, grad_out, weight, fh, fl, ih, filt,
    sbuf, rbuf, g_first, g_second, v_spec, m_spec, s_spec, f_spec, product,
    first_conv, grad_gated, xt,
    w_part, w_pair, w_sum, w_plane, w_tiles, w_ring,
    f_part, f_pair, f_sum, f_plane, f_send, f_recv, f_turned,
    in_sem, z_send, z_recv, pair_send, pair_recv, plane_send, plane_recv,
    ring_send, ring_recv, own_send, own_recv,
):
    doc = lax.axis_index("dp")
    pos = lax.axis_index("ctx")
    core = lax.rem(doc, 2)
    chip = lax.div(doc, 2)

    barrier = pltpu.get_barrier_semaphore()
    for o in range(1, CTX):
        pl.semaphore_signal(barrier, inc=1, device_id=(doc, lax.rem(pos + o, CTX)), device_id_type=MESH)
    pl.semaphore_signal(barrier, inc=1, device_id=(2 * chip + 1 - core, pos), device_id_type=MESH)
    for o in range(1, CHIPS):
        peer = 2 * lax.rem(chip + o, CHIPS) + core
        pl.semaphore_signal(barrier, inc=1, device_id=(peer, pos), device_id_type=MESH)

    column = pl.multiple_of(lax.div(pos, 2) * 128, 128)
    loads = {}
    for i, (name, src, dst) in enumerate((
        ("value", value_hbm, value),
        ("filt", filters_hbm.at[:, :, pl.ds(column, 128)], filt),
        ("fh", fh_hbm, fh),
        ("fl", fl_hbm, fl),
        ("gate_one", gate_one_hbm, gate_one),
        ("grad_out", grad_out_hbm, grad_out),
        ("weight", weight_hbm, weight),
        ("gate_two", gate_two_hbm, gate_two),
        ("ih", ih_hbm, ih),
    )):
        loads[name] = pltpu.make_async_copy(src, dst, in_sem.at[i])
        loads[name].start()

    def pack_rows(slot, tile_of):
        for p in range(4):
            first, second = mix(tile_of(0, p), tile_of(1, p))
            sbuf[slot, 2 * p] = first.astype(BF16)
            sbuf[slot, 2 * p + 1] = second.astype(BF16)
        rbuf[slot, pos] = sbuf[slot, pos]

    def pack_blocks(slot, tiles):
        for t in range(2):
            for h in range(2):
                part = tiles[t][128 * h : 128 * h + 128]
                first, second = mix(part[:64], part[64:])
                sbuf[slot, 4 * t + h] = first.astype(BF16)
                sbuf[slot, 4 * t + 2 + h] = second.astype(BF16)
        rbuf[slot, pos] = sbuf[slot, pos]

    def ring_copy(slot, to, at):
        return pltpu.make_async_remote_copy(
            src_ref=sbuf.at[slot, to],
            dst_ref=rbuf.at[slot, at],
            send_sem=z_send.at[slot, to],
            recv_sem=z_recv.at[slot, at],
            device_id=(doc, to),
            device_id_type=MESH,
        )

    def ring_start(slot):
        for o in (4, 3, 5, 2, 6, 1, 7):
            ring_copy(slot, lax.rem(pos + o, CTX), pos).start()

    def ring_wait(slot):
        for o in (1, 7, 2, 6, 3, 5, 4):
            src = lax.rem(pos + o, CTX)
            ring_copy(slot, src, src).wait_recv()

    def rows_tile(ref):
        return lambda h, p: ref[64 * h : 64 * h + 64, 128 * p : 128 * p + 128].astype(F32)

    loads["value"].wait()
    pack_rows(0, rows_tile(value))
    pl.semaphore_wait(barrier, CTX + CHIPS - 1)
    ring_start(0)

    def forward(spec):
        block = xt[...]
        spec[...] = jnp.dot(fh[...], block, preferred_element_type=F32) + jnp.dot(
            fl[...], block, preferred_element_type=F32
        )

    def inverse(slot=0):
        return jnp.dot(ih[...], product[slot], preferred_element_type=F32)

    def load(spec, r):
        a = spec[pl.ds(r, CHUNK), :]
        b = spec[pl.ds(BINS + r, CHUNK), :]
        return (a[:, :128], b[:, :128]), (a[:, 128:], b[:, 128:])

    def store(slot, r, low_blocks, high_blocks):
        for part in range(2):
            for t, block in enumerate((low_blocks, high_blocks)):
                product[slot, pl.ds(part * BINS + r, CHUNK), 128 * t : 128 * t + 128] = block[part].astype(BF16)

    def both(x):
        return tuple(turn(part) for part in x)

    def pick(a, b):
        low = lanes_low(CHUNK)
        return tuple(jnp.where(low, x, y) for x, y in zip(a, b))

    def low_only(x):
        return pick(x, (jnp.zeros_like(x[0]),) * 2)

    def high_only(x):
        return pick((jnp.zeros_like(x[0]),) * 2, x)

    def times(a, b):
        return a[0] * b[0] - a[1] * b[1], a[0] * b[1] + a[1] * b[0]

    def conj_times(a, b):
        return a[0] * b[0] + a[1] * b[1], a[0] * b[1] - a[1] * b[0]

    def plus(*terms):
        return sum(t[0] for t in terms[1:]) + terms[0][0], sum(t[1] for t in terms[1:]) + terms[0][1]

    def chunks(body):
        for half, sign in ((0, 1.0), (1, -1.0)):

            def step(i, carry):
                body(pl.multiple_of(half * (BINS // 2) + i * CHUNK, CHUNK), sign)
                return carry

            lax.fori_loop(0, BINS // 2 // CHUNK, step, 0, unroll=UNROLL)

    def spread(g01, g23):
        t01, t23 = both(g01), both(g23)
        return pick(g01, t01), pick(t01, g01), pick(g23, t23), t01, t23

    def convolve(filter_spec, data_spec):
        def body(r, sign):
            g01, g23 = load(filter_spec, r)
            x01, x23 = load(data_spec, r)
            h0, h1, h2, _, _ = spread(g01, g23)
            x10, x32 = both(x01), both(x23)
            x12 = pick(x10, x32)
            out01 = plus(times(h0, x01), times(high_only(g01), x10))
            out23 = plus(times(h0, x23), times(h1, x12), times(h2, x01), times(high_only(g23), x10))
            store(0, r, out01, out23)

        chunks(body)

    def correlate(filter_spec, data_spec, windows, slot=0):
        def body(r, sign):
            g01, g23 = load(filter_spec, r)
            y01, y23 = load(data_spec, r)
            if windows:
                t01, t23 = both(y01), both(y23)
                n01, n23 = pick(t01, t23), low_only(t23)
                y01 = (y01[0] + sign * n01[1], y01[1] - sign * n01[0])
                y23 = (y23[0] + sign * n23[1], y23[1] - sign * n23[0])
            h0, h1, h2, t01, t23 = spread(g01, g23)
            y10, y32 = both(y01), both(y23)
            y12 = pick(y10, y32)
            out01 = plus(
                conj_times(h0, y01), conj_times(h1, y12), conj_times(h2, y23), conj_times(low_only(t23), y32)
            )
            out23 = plus(conj_times(h0, y23), conj_times(low_only(t01), y32))
            store(slot, r, out01, out23)

        chunks(body)

    odd = lax.rem(pos, 2) == 1

    def filter_windows(which, spec):
        for t in range(2):
            lag_tiles = []
            for k in (2 * t, 2 * t + 1):
                tile = filt[which, BLK * k : BLK * k + BLK, :].astype(F32)
                lag_tiles.append(jnp.where(odd, turn(tile), tile))
            xt[:, 128 * t : 128 * t + 128] = mix(*lag_tiles)[0].astype(BF16)
        forward(spec)

        def window(r, sign):
            h01, h23 = load(spec, r)
            t01, t23 = both(h01), both(h23)
            b01, b23 = high_only(t01), pick(t01, t23)
            for t, (h, b) in enumerate(((h01, b01), (h23, b23))):
                spec[pl.ds(r, CHUNK), 128 * t : 128 * t + 128] = h[0] - sign * b[1]
                spec[pl.ds(BINS + r, CHUNK), 128 * t : 128 * t + 128] = h[1] + sign * b[0]

        chunks(window)

    for name in ("filt", "fh", "fl", "gate_one"):
        loads[name].wait()
    pack_rows(1, rows_tile(gate_one))
    filter_windows(0, g_first)
    ring_start(1)
    for name in ("grad_out", "weight", "gate_two", "ih"):
        loads[name].wait()
    grad_gated[...] = lax.dot_general(
        grad_out[...], weight[...], (((1,), (1,)), ((), ())), preferred_element_type=F32
    )
    pack_rows(
        2,
        lambda h, p: (
            grad_gated[64 * h : 64 * h + 64, 128 * p : 128 * p + 128]
            * gate_two[64 * h : 64 * h + 64, 128 * p : 128 * p + 128].astype(F32)
        ).astype(BF16).astype(F32),
    )
    ring_start(2)
    filter_windows(1, g_second)

    def arrived(slot, t, h):
        return mix(rbuf[slot, 4 * t + h].astype(F32), rbuf[slot, 4 * t + 2 + h].astype(F32))

    def to_columns(slot, scale=None):
        for t in range(2):
            for h in range(2):
                for half, part in enumerate(arrived(slot, t, h)):
                    where = (
                        slice(128 * h + 64 * half, 128 * h + 64 * half + 64),
                        slice(128 * t, 128 * t + 128),
                    )
                    if scale is not None:
                        part = part * scale[where]
                    xt[where] = part.astype(BF16)

    def split_tiles(x):
        return x[:, :128], x[:, 128:]

    ring_wait(0)
    to_columns(0)
    forward(v_spec)
    convolve(g_first, v_spec)
    first_conv[...] = inverse()
    ring_wait(1)
    to_columns(1, first_conv)
    forward(m_spec)
    convolve(g_second, m_spec)
    pack_blocks(3, split_tiles(inverse()))
    ring_start(3)

    ring_wait(2)
    to_columns(2)
    forward(s_spec)
    correlate(g_second, s_spec, False)
    grad_mixed = inverse()
    pack_blocks(4, split_tiles(grad_mixed * first_conv[...]))
    ring_start(4)
    to_columns(1, grad_mixed)
    forward(f_spec)

    def pair_copy(index, src, dst):
        return pltpu.make_async_remote_copy(
            src_ref=src.at[1 - core],
            dst_ref=dst,
            send_sem=pair_send.at[index],
            recv_sem=pair_recv.at[index],
            device_id=(2 * chip + 1 - core, pos),
            device_id_type=MESH,
        )

    def plane_copy(index, src, dst, to, at):
        return pltpu.make_async_remote_copy(
            src_ref=src.at[to],
            dst_ref=dst.at[at],
            send_sem=plane_send.at[index, to],
            recv_sem=plane_recv.at[index, at],
            device_id=(2 * to + core, pos),
            device_id_type=MESH,
        )

    def plane_start(index, src, dst):
        for o in range(1, CHIPS):
            plane_copy(index, src, dst, lax.rem(chip + o, CHIPS), chip).start()

    def plane_wait(index, src, dst):
        for o in range(1, CHIPS):
            at = lax.rem(chip + o, CHIPS)
            plane_copy(index, src, dst, at, at).wait_recv()

    correlate(v_spec, f_spec, True, 0)
    correlate(m_spec, s_spec, True, 1)
    for which in range(2):
        lags = inverse(which).astype(BF16)
        for h in range(2):
            for t in range(2):
                for g in range(8):
                    row = 128 * h + 16 * g
                    f_part[g % 2, 4 * (2 * h + t) + g // 2, 16 * which : 16 * which + 16, :] = lags[
                        row : row + 16, 128 * t : 128 * t + 128
                    ]
    f_pair_copy = pair_copy(0, f_part, f_pair)
    f_pair_copy.start()

    def row_tile(slot, p):
        return mix(rbuf[slot, 2 * p].astype(F32), rbuf[slot, 2 * p + 1].astype(F32))

    ring_wait(3)
    for p in range(4):
        for half, part in enumerate(row_tile(3, p)):
            where = (slice(64 * half, 64 * half + 64), slice(128 * p, 128 * p + 128))
            grad_gate_two[where] = (grad_gated[where] * part).astype(BF16)
            grad_gated[where] = (gate_two[where].astype(F32) * part).astype(BF16).astype(F32)
    gated = grad_gated[...].astype(BF16)
    gated_t = grad_gated[...].T.astype(BF16)
    for c in range(4):
        part = jnp.dot(
            gated_t[128 * c : 128 * c + 128], grad_out[...], preferred_element_type=F32
        ).astype(BF16)
        for i in range(8):
            row = 16 * (4 * c + i // 2)
            w_part[i % 2, 4 * c + i // 2] = part[16 * i : 16 * i + 16]
    w_pair_copy = pair_copy(1, w_part, w_pair)
    w_pair_copy.start()
    f_pair_copy.wait_recv()
    f_sum[...] = (f_part[core].astype(F32) + f_pair[...].astype(F32)).astype(BF16)
    plane_start(0, f_sum, f_plane)
    f_plane[chip] = f_sum[chip]
    correlate(g_first, f_spec, False)
    pack_blocks(5, split_tiles(inverse()))
    ring_start(5)
    w_pair_copy.wait_recv()
    w_sum[...] = (w_part[core].astype(F32) + w_pair[...].astype(F32)).astype(BF16)
    plane_start(1, w_sum, w_plane)
    w_plane[chip] = w_sum[chip]
    mixed[...] = jnp.dot(gated, weight[...], preferred_element_type=F32).astype(BF16)

    for slot, out in ((4, grad_gate_one), (5, grad_value)):
        ring_wait(slot)
        for p in range(4):
            for half, part in enumerate(row_tile(slot, p)):
                out[64 * half : 64 * half + 64, 128 * p : 128 * p + 128] = part.astype(BF16)

    scale = 1.0 / 32

    plane_wait(0, f_sum, f_plane)
    f_send[...] = jnp.sum(f_plane[...].astype(F32), axis=0) * scale
    piece_h = lax.div(doc, 16)
    piece_t = lax.rem(lax.div(doc, 8), 2)
    piece_g = lax.rem(doc, 8)

    def owner(i):
        return 4 * pos + i % 4, 2 * (2 * piece_t + i // 4) + piece_h

    def own_copy(i, at):
        to_doc, to_pos = owner(i)
        return pltpu.make_async_remote_copy(
            src_ref=f_send,
            dst_ref=f_recv.at[at],
            send_sem=own_send.at[i],
            recv_sem=own_recv.at[at],
            device_id=(to_doc, to_pos),
            device_id_type=MESH,
        )

    def is_self(i):
        to_doc, to_pos = owner(i)
        return jnp.logical_and(to_doc == doc, to_pos == pos)

    for i in range(8):

        @pl.when(jnp.logical_not(is_self(i)))
        def _():
            own_copy(i, piece_g).start()

        @pl.when(is_self(i))
        def _():
            f_recv[piece_g] = f_send[...]

    def tile_copy(to, at):
        return pltpu.make_async_remote_copy(
            src_ref=w_tiles.at[lax.div(to, 2)],
            dst_ref=w_ring.at[at],
            send_sem=ring_send.at[to],
            recv_sem=ring_recv.at[at],
            device_id=(doc, to),
            device_id_type=MESH,
        )

    plane_wait(1, w_sum, w_plane)
    w_total = jnp.sum(w_plane[...].astype(F32), axis=0).astype(BF16)
    for p in range(4):
        w_tiles[p] = w_total[:, 128 * p : 128 * p + 128]
    for o in (4, 3, 5, 2, 6, 1, 7):
        tile_copy(lax.rem(pos + o, CTX), pos).start()
    w_ring[pos] = w_tiles[lax.div(pos, 2)]
    for o in range(1, CTX):
        src = lax.rem(pos + o, CTX)
        tile_copy(src, src).wait_recv()
    total = jnp.sum(w_ring[...].astype(F32), axis=0) * scale
    weight_grad[...] = jnp.where(odd, turn(total), total)[:, :64]

    from_pos = lax.div(doc, 4)
    first_doc = 16 * lax.rem(pos, 2) + 8 * lax.div(pos, 4)
    for g in range(8):

        @pl.when(jnp.logical_not(jnp.logical_and(from_pos == pos, first_doc + g == doc)))
        def _():
            own_copy(0, g).wait_recv()

    group = 4 * lax.rem(lax.div(pos, 2), 2) + lax.rem(doc, 4)
    for which in range(2):
        rows = f_recv[:, 16 * which : 16 * which + 16, :].reshape(ROWS, 128)
        f_turned[which] = rows.T
    for which in range(2):
        filter_grad[which] = f_turned[which, pl.ds(pl.multiple_of(16 * group, 16), 16), :]

    for slot in range(6):
        for o in range(1, CTX):
            ring_copy(slot, lax.rem(pos + o, CTX), pos).wait_send()
    f_pair_copy.wait_send()
    w_pair_copy.wait_send()
    for index, src, dst in ((0, f_sum, f_plane), (1, w_sum, w_plane)):
        for o in range(1, CHIPS):
            plane_copy(index, src, dst, lax.rem(chip + o, CHIPS), chip).wait_send()
    for o in range(1, CTX):
        tile_copy(lax.rem(pos + o, CTX), pos).wait_send()

    for i in range(8):

        @pl.when(jnp.logical_not(is_self(i)))
        def _():
            own_copy(i, piece_g).wait_send()


def finish(*refs):
    sems = refs[12]
    copies = [pltpu.make_async_copy(refs[i], refs[6 + i], sems.at[i]) for i in range(6)]
    for copy in copies:
        copy.start()
    for copy in copies:
        copy.wait()


def on_device(value, gate_one, gate_two, filters, out_weight, grad_out):
    vmem = pl.BlockSpec(memory_space=pltpu.VMEM)
    anywhere = pl.BlockSpec(memory_space=pl.ANY)
    stream = pltpu.VMEM((ROWS, WIDTH), BF16)
    table = pltpu.VMEM((2 * BINS, 256), BF16)
    spectrum = pltpu.VMEM((2 * BINS, 256), F32)
    dma = pltpu.SemaphoreType.DMA
    shapes = [((ROWS, WIDTH), BF16)] * 4 + [((2, 16, ROWS), F32), ((16, 64), F32)]
    outs = pl.pallas_call(
        kernel,
        out_shape=tuple(pltpu.VMEM(*shape) for shape in shapes),
        in_specs=[anywhere] * 9,
        out_specs=[vmem] * 6,
        scratch_shapes=[
            stream, stream, stream, stream,
            pltpu.VMEM((WIDTH, WIDTH), BF16),
            table, table,
            pltpu.VMEM((BLK, 2 * BINS), BF16),
            pltpu.VMEM((2, 1024, 128), BF16),
            pltpu.VMEM((6, CTX, 64, 128), BF16),
            pltpu.VMEM((6, CTX, 64, 128), BF16),
            spectrum, spectrum, spectrum, spectrum, spectrum, spectrum,
            pltpu.VMEM((2, 2 * BINS, 256), BF16),
            pltpu.VMEM((BLK, 256), F32),
            pltpu.VMEM((ROWS, WIDTH), F32),
            pltpu.VMEM((BLK, 256), BF16),
            pltpu.VMEM((2, CHIPS, 16, WIDTH), BF16),
            pltpu.VMEM((CHIPS, 16, WIDTH), BF16),
            pltpu.VMEM((CHIPS, 16, WIDTH), BF16),
            pltpu.VMEM((CHIPS, 16, WIDTH), BF16),
            pltpu.VMEM((4, 16, 128), BF16),
            pltpu.VMEM((CTX, 16, 128), BF16),
            pltpu.VMEM((2, CHIPS, 32, 128), BF16),
            pltpu.VMEM((CHIPS, 32, 128), BF16),
            pltpu.VMEM((CHIPS, 32, 128), BF16),
            pltpu.VMEM((CHIPS, 32, 128), BF16),
            pltpu.VMEM((32, 128), F32),
            pltpu.VMEM((8, 32, 128), F32),
            pltpu.VMEM((2, ROWS, 128), F32),
            dma((9,)),
            dma((6, CTX)),
            dma((6, CTX)),
            dma((2,)),
            dma((2,)),
            dma((2, CHIPS)),
            dma((2, CHIPS)),
            dma((CTX,)),
            dma((CTX,)),
            dma((8,)),
            dma((8,)),
        ],
        compiler_params=pltpu.CompilerParams(collective_id=0, has_side_effects=True),
    )(
        value[0], gate_one[0], gate_two[0], grad_out[0], filters, out_weight,
        *(jnp.asarray(table) for table in tables()),
    )
    outs = pl.pallas_call(
        finish,
        out_shape=tuple(jax.ShapeDtypeStruct(*shape) for shape in shapes),
        in_specs=[vmem] * 6,
        out_specs=[anywhere] * 6,
        scratch_shapes=[dma((6,))],
    )(*outs)
    mixed, grad_value, grad_gate_one, grad_gate_two, filter_grad, weight_grad = outs
    return (
        mixed[None], grad_value[None], grad_gate_one[None], grad_gate_two[None],
        jnp.swapaxes(filter_grad, 1, 2), weight_grad,
    )


def solution(mesh):
    stream = P("dp", "ctx", None)
    return jax.shard_map(
        on_device,
        mesh=mesh,
        in_specs=(stream, stream, stream, P(), P(), stream),
        out_specs=(stream, stream, stream, stream, P(None, "ctx", "dp"), P("dp", "ctx")),
        check_vma=False,
    )
```

```python
import numpy as np

import jax
import jax.numpy as jnp
from jax import lax
from jax.experimental import pallas as pl
from jax.experimental.pallas import tpu as pltpu
from jax.sharding import PartitionSpec as P

F32 = jnp.float32
BF16 = jnp.bfloat16
MESH = pl.DeviceIdType.MESH

CTX = 8
CHIPS = 16
WIDTH = 512
ROWS = 128
BLK = 256
BINS = 256
CHUNK = 16
UNROLL = 8
PLANE = sorted(
    ((dy, dx) for dy in range(4) for dx in range(4) if dy or dx),
    key=lambda d: -sum(min(step, 4 - step) for step in d),
)


def tables():
    bins = np.concatenate([np.arange(0, BINS, 2), np.arange(1, BINS, 2)])
    angle = 2.0 * np.pi * (bins[:, None] + 0.5) * np.arange(BLK)[None, :] / (2 * BLK)
    forward = np.concatenate([np.cos(angle), -np.sin(angle)], axis=0)
    inverse = forward.T / BINS

    def split(table):
        high = table.astype(BF16)
        low = (table - high.astype(np.float64)).astype(BF16)
        return high, low

    return split(forward) + split(inverse)[:1]


def lanes_low(rows):
    return lax.broadcasted_iota(jnp.int32, (rows, 128), 1) < 64


def turn(x, shift=64):
    return pltpu.roll(x, shift, 1)


def mix(a, b):
    low = lanes_low(a.shape[0])
    return jnp.where(low, a, turn(b)), jnp.where(low, turn(a), b)


def kernel(
    value_hbm, gate_one_hbm, gate_two_hbm, grad_out_hbm, filters_hbm, weight_hbm, fh_hbm, fl_hbm, ih_hbm,
    mixed, grad_value, grad_gate_one, grad_gate_two, filter_grad, weight_grad,
    value, gate_one, gate_two, grad_out, weight, fh, fl, ih, filt,
    sbuf, rbuf, g_first, g_second, v_spec, m_spec, s_spec, f_spec, product,
    first_conv, grad_gated, xt,
    w_part, w_pair, w_sum, w_plane, w_tiles, w_ring,
    f_part, f_pair, f_sum, f_plane, f_send, f_recv, f_turned,
    in_sem, z_send, z_recv, pair_send, pair_recv, plane_send, plane_recv,
    last_send, last_recv, own_send, own_recv,
):
    doc = lax.axis_index("dp")
    pos = lax.axis_index("ctx")
    core = lax.rem(doc, 2)
    chip = lax.div(doc, 2)

    barrier = pltpu.get_barrier_semaphore()
    for o in range(1, CTX):
        pl.semaphore_signal(barrier, inc=1, device_id=(doc, lax.rem(pos + o, CTX)), device_id_type=MESH)
    pl.semaphore_signal(barrier, inc=1, device_id=(2 * chip + 1 - core, pos), device_id_type=MESH)
    for o in range(1, CHIPS):
        peer = 2 * lax.rem(chip + o, CHIPS) + core
        pl.semaphore_signal(barrier, inc=1, device_id=(peer, pos), device_id_type=MESH)

    column = pl.multiple_of(lax.div(pos, 2) * 128, 128)
    loads = {}
    for i, (name, src, dst) in enumerate((
        ("value", value_hbm, value),
        ("filt", filters_hbm.at[:, :, pl.ds(column, 128)], filt),
        ("fh", fh_hbm, fh),
        ("fl", fl_hbm, fl),
        ("gate_one", gate_one_hbm, gate_one),
        ("grad_out", grad_out_hbm, grad_out),
        ("weight", weight_hbm, weight),
        ("gate_two", gate_two_hbm, gate_two),
        ("ih", ih_hbm, ih),
    )):
        loads[name] = pltpu.make_async_copy(src, dst, in_sem.at[i])
        loads[name].start()

    def pack_rows(slot, tile_of):
        for p in range(4):
            first, second = mix(tile_of(0, p), tile_of(1, p))
            sbuf[slot, 2 * p] = first.astype(BF16)
            sbuf[slot, 2 * p + 1] = second.astype(BF16)
        rbuf[slot, pos] = sbuf[slot, pos]

    def pack_blocks(slot, tiles):
        for t in range(2):
            for h in range(2):
                part = tiles[t][128 * h : 128 * h + 128]
                first, second = mix(part[:64], part[64:])
                sbuf[slot, 4 * t + h] = first.astype(BF16)
                sbuf[slot, 4 * t + 2 + h] = second.astype(BF16)
        rbuf[slot, pos] = sbuf[slot, pos]

    def ring_copy(slot, to, at):
        return pltpu.make_async_remote_copy(
            src_ref=sbuf.at[slot, to],
            dst_ref=rbuf.at[slot, at],
            send_sem=z_send.at[slot],
            recv_sem=z_recv.at[slot],
            device_id=(doc, to),
            device_id_type=MESH,
        )

    def ring_start(slot):
        for o in (4, 3, 5, 2, 6, 1, 7):
            ring_copy(slot, lax.rem(pos + o, CTX), pos).start()

    def ring_all(slot):
        most = pl.ds(0, CTX - 1)
        return pltpu.make_async_remote_copy(
            src_ref=sbuf.at[slot, most],
            dst_ref=rbuf.at[slot, most],
            send_sem=z_send.at[slot],
            recv_sem=z_recv.at[slot],
            device_id=(doc, lax.rem(pos + 1, CTX)),
            device_id_type=MESH,
        )

    def ring_wait(slot):
        ring_all(slot).wait_recv()

    def rows_tile(ref):
        return lambda h, p: ref[64 * h : 64 * h + 64, 128 * p : 128 * p + 128].astype(F32)

    loads["value"].wait()
    pack_rows(0, rows_tile(value))
    pl.semaphore_wait(barrier, CTX + CHIPS - 1)
    ring_start(0)

    def forward(spec):
        block = xt[...]
        spec[...] = jnp.dot(fh[...], block, preferred_element_type=F32) + jnp.dot(
            fl[...], block, preferred_element_type=F32
        )

    def inverse(slot=0):
        return jnp.dot(ih[...], product[slot], preferred_element_type=F32)

    def load(spec, r):
        a = spec[pl.ds(r, CHUNK), :]
        b = spec[pl.ds(BINS + r, CHUNK), :]
        return (a[:, :128], b[:, :128]), (a[:, 128:], b[:, 128:])

    def store(slot, r, low_blocks, high_blocks):
        for part in range(2):
            for t, block in enumerate((low_blocks, high_blocks)):
                product[slot, pl.ds(part * BINS + r, CHUNK), 128 * t : 128 * t + 128] = block[part].astype(BF16)

    def both(x):
        return tuple(turn(part) for part in x)

    def pick(a, b):
        low = lanes_low(CHUNK)
        return tuple(jnp.where(low, x, y) for x, y in zip(a, b))

    def low_only(x):
        return pick(x, (jnp.zeros_like(x[0]),) * 2)

    def high_only(x):
        return pick((jnp.zeros_like(x[0]),) * 2, x)

    def times(a, b):
        return a[0] * b[0] - a[1] * b[1], a[0] * b[1] + a[1] * b[0]

    def conj_times(a, b):
        return a[0] * b[0] + a[1] * b[1], a[0] * b[1] - a[1] * b[0]

    def plus(*terms):
        return sum(t[0] for t in terms[1:]) + terms[0][0], sum(t[1] for t in terms[1:]) + terms[0][1]

    def chunks(body):
        for half, sign in ((0, 1.0), (1, -1.0)):

            def step(i, carry):
                body(pl.multiple_of(half * (BINS // 2) + i * CHUNK, CHUNK), sign)
                return carry

            lax.fori_loop(0, BINS // 2 // CHUNK, step, 0, unroll=UNROLL)

    def spread(g01, g23):
        t01, t23 = both(g01), both(g23)
        return pick(g01, t01), pick(t01, g01), pick(g23, t23), t01, t23

    def convolve(filter_spec, data_spec):
        def body(r, sign):
            g01, g23 = load(filter_spec, r)
            x01, x23 = load(data_spec, r)
            h0, h1, h2, _, _ = spread(g01, g23)
            x10, x32 = both(x01), both(x23)
            x12 = pick(x10, x32)
            out01 = plus(times(h0, x01), times(high_only(g01), x10))
            out23 = plus(times(h0, x23), times(h1, x12), times(h2, x01), times(high_only(g23), x10))
            store(0, r, out01, out23)

        chunks(body)

    def correlate(filter_spec, data_spec, windows, slot=0):
        def body(r, sign):
            g01, g23 = load(filter_spec, r)
            y01, y23 = load(data_spec, r)
            if windows:
                t01, t23 = both(y01), both(y23)
                n01, n23 = pick(t01, t23), low_only(t23)
                y01 = (y01[0] + sign * n01[1], y01[1] - sign * n01[0])
                y23 = (y23[0] + sign * n23[1], y23[1] - sign * n23[0])
            h0, h1, h2, t01, t23 = spread(g01, g23)
            y10, y32 = both(y01), both(y23)
            y12 = pick(y10, y32)
            out01 = plus(
                conj_times(h0, y01), conj_times(h1, y12), conj_times(h2, y23), conj_times(low_only(t23), y32)
            )
            out23 = plus(conj_times(h0, y23), conj_times(low_only(t01), y32))
            store(slot, r, out01, out23)

        chunks(body)

    odd = lax.rem(pos, 2) == 1

    def filter_windows(which, spec):
        for t in range(2):
            lag_tiles = []
            for k in (2 * t, 2 * t + 1):
                tile = filt[which, BLK * k : BLK * k + BLK, :].astype(F32)
                lag_tiles.append(jnp.where(odd, turn(tile), tile))
            xt[:, 128 * t : 128 * t + 128] = mix(*lag_tiles)[0].astype(BF16)
        forward(spec)

        def window(r, sign):
            h01, h23 = load(spec, r)
            t01, t23 = both(h01), both(h23)
            b01, b23 = high_only(t01), pick(t01, t23)
            for t, (h, b) in enumerate(((h01, b01), (h23, b23))):
                spec[pl.ds(r, CHUNK), 128 * t : 128 * t + 128] = h[0] - sign * b[1]
                spec[pl.ds(BINS + r, CHUNK), 128 * t : 128 * t + 128] = h[1] + sign * b[0]

        chunks(window)

    for name in ("filt", "fh", "fl", "gate_one"):
        loads[name].wait()
    pack_rows(1, rows_tile(gate_one))
    filter_windows(0, g_first)
    ring_start(1)
    for name in ("grad_out", "weight", "gate_two", "ih"):
        loads[name].wait()
    grad_gated[...] = lax.dot_general(
        grad_out[...], weight[...], (((1,), (1,)), ((), ())), preferred_element_type=F32
    )
    pack_rows(
        2,
        lambda h, p: (
            grad_gated[64 * h : 64 * h + 64, 128 * p : 128 * p + 128]
            * gate_two[64 * h : 64 * h + 64, 128 * p : 128 * p + 128].astype(F32)
        ).astype(BF16).astype(F32),
    )
    ring_start(2)
    filter_windows(1, g_second)

    def arrived(slot, t, h):
        return mix(rbuf[slot, 4 * t + h].astype(F32), rbuf[slot, 4 * t + 2 + h].astype(F32))

    def to_columns(slot, scale=None):
        for t in range(2):
            for h in range(2):
                for half, part in enumerate(arrived(slot, t, h)):
                    where = (
                        slice(128 * h + 64 * half, 128 * h + 64 * half + 64),
                        slice(128 * t, 128 * t + 128),
                    )
                    if scale is not None:
                        part = part * scale[where]
                    xt[where] = part.astype(BF16)

    def split_tiles(x):
        return x[:, :128], x[:, 128:]

    ring_wait(0)
    to_columns(0)
    forward(v_spec)
    convolve(g_first, v_spec)
    first_conv[...] = inverse()
    ring_wait(1)
    to_columns(1, first_conv)
    forward(m_spec)
    convolve(g_second, m_spec)
    pack_blocks(3, split_tiles(inverse()))
    ring_start(3)

    ring_wait(2)
    to_columns(2)
    forward(s_spec)
    correlate(g_second, s_spec, False)
    grad_mixed = inverse()
    pack_blocks(4, split_tiles(grad_mixed * first_conv[...]))
    ring_start(4)
    to_columns(1, grad_mixed)
    forward(f_spec)

    def pair_copy(index, src, dst):
        return pltpu.make_async_remote_copy(
            src_ref=src.at[1 - core],
            dst_ref=dst,
            send_sem=pair_send.at[index],
            recv_sem=pair_recv.at[index],
            device_id=(2 * chip + 1 - core, pos),
            device_id_type=MESH,
        )

    def plane_start(index, src, dst):
        row, col = lax.div(chip, 4), lax.rem(chip, 4)
        for dy, dx in PLANE:
            to = 4 * lax.rem(row + dy, 4) + lax.rem(col + dx, 4)
            pltpu.make_async_remote_copy(
                src_ref=src.at[to],
                dst_ref=dst.at[chip],
                send_sem=plane_send.at[index],
                recv_sem=plane_recv.at[index],
                device_id=(2 * to + core, pos),
                device_id_type=MESH,
            ).start()
        dst[chip] = src[chip]

    def plane_all(index, src, dst):
        most = pl.ds(0, CHIPS - 1)
        return pltpu.make_async_remote_copy(
            src_ref=src.at[most],
            dst_ref=dst.at[most],
            send_sem=plane_send.at[index],
            recv_sem=plane_recv.at[index],
            device_id=(2 * lax.rem(chip + 1, CHIPS) + core, pos),
            device_id_type=MESH,
        )

    correlate(v_spec, f_spec, True, 0)
    correlate(m_spec, s_spec, True, 1)
    for which in range(2):
        lags = inverse(which).astype(BF16)
        for h in range(2):
            for t in range(2):
                for g in range(8):
                    row = 128 * h + 16 * g
                    f_part[g % 2, 4 * (2 * h + t) + g // 2, 16 * which : 16 * which + 16, :] = lags[
                        row : row + 16, 128 * t : 128 * t + 128
                    ]
    f_pair_copy = pair_copy(0, f_part, f_pair)
    f_pair_copy.start()

    def row_tile(slot, p):
        return mix(rbuf[slot, 2 * p].astype(F32), rbuf[slot, 2 * p + 1].astype(F32))

    ring_wait(3)
    for p in range(4):
        for half, part in enumerate(row_tile(3, p)):
            where = (slice(64 * half, 64 * half + 64), slice(128 * p, 128 * p + 128))
            grad_gate_two[where] = (grad_gated[where] * part).astype(BF16)
            grad_gated[where] = (gate_two[where].astype(F32) * part).astype(BF16).astype(F32)
    gated = grad_gated[...].astype(BF16)
    gated_t = grad_gated[...].T.astype(BF16)
    for c in range(4):
        part = jnp.dot(
            gated_t[128 * c : 128 * c + 128], grad_out[...], preferred_element_type=F32
        ).astype(BF16)
        for i in range(8):
            row = 16 * (4 * c + i // 2)
            w_part[i % 2, 4 * c + i // 2] = part[16 * i : 16 * i + 16]
    w_pair_copy = pair_copy(1, w_part, w_pair)
    w_pair_copy.start()
    f_pair_copy.wait_recv()
    f_sum[...] = (f_part[core].astype(F32) + f_pair[...].astype(F32)).astype(BF16)
    plane_start(0, f_sum, f_plane)
    correlate(g_first, f_spec, False)
    pack_blocks(5, split_tiles(inverse()))
    ring_start(5)
    w_pair_copy.wait_recv()
    w_sum[...] = (w_part[core].astype(F32) + w_pair[...].astype(F32)).astype(BF16)
    plane_start(1, w_sum, w_plane)

    def deliver(slot, out):
        ring_wait(slot)
        for p in range(4):
            for half, part in enumerate(row_tile(slot, p)):
                out[64 * half : 64 * half + 64, 128 * p : 128 * p + 128] = part.astype(BF16)

    deliver(4, grad_gate_one)
    mixed[...] = jnp.dot(gated, weight[...], preferred_element_type=F32).astype(BF16)

    scale = 1.0 / 32

    plane_all(0, f_sum, f_plane).wait_recv()
    total = jnp.sum(f_plane[...].astype(F32), axis=0) * scale
    for k, part in enumerate(mix(total[:16], total[16:])):
        f_send[k] = part.astype(BF16)
    piece_h = lax.div(doc, 16)
    piece_t = lax.rem(lax.div(doc, 8), 2)
    piece_g = lax.rem(doc, 8)
    first_doc = 16 * lax.rem(pos, 2) + 8 * lax.div(pos, 4)
    owns_piece = jnp.logical_and(lax.div(doc, 4) == pos, first_doc + piece_g == doc)

    for i in range(8):
        to_doc, to_pos = 4 * pos + i % 4, 2 * (2 * piece_t + i // 4) + piece_h
        is_self = jnp.logical_and(to_doc == doc, to_pos == pos)

        @pl.when(jnp.logical_not(is_self))
        def _():
            pltpu.make_async_remote_copy(
                src_ref=f_send.at[i // 4],
                dst_ref=f_recv.at[piece_g],
                send_sem=own_send,
                recv_sem=own_recv,
                device_id=(to_doc, to_pos),
                device_id_type=MESH,
            ).start()

        @pl.when(is_self)
        def _():
            f_recv[piece_g] = f_send[i // 4]

    def own_all(count):
        return pltpu.make_async_remote_copy(
            src_ref=f_recv.at[pl.ds(0, count)],
            dst_ref=f_recv.at[pl.ds(0, count)],
            send_sem=own_send,
            recv_sem=own_recv,
            device_id=(doc, lax.rem(pos + 1, CTX)),
            device_id_type=MESH,
        )

    plane_all(1, w_sum, w_plane).wait_recv()
    w_total = jnp.sum(w_plane[...].astype(F32), axis=0).astype(BF16)
    for p in range(4):
        w_tiles[p] = w_total[:, 128 * p : 128 * p + 128]
    for o in (4, 3, 5, 2, 6, 1, 7):
        to = lax.rem(pos + o, CTX)
        pltpu.make_async_remote_copy(
            src_ref=w_tiles.at[lax.div(to, 2)],
            dst_ref=w_ring.at[pos],
            send_sem=last_send,
            recv_sem=last_recv,
            device_id=(doc, to),
            device_id_type=MESH,
        ).start()
    w_ring[pos] = w_tiles[lax.div(pos, 2)]
    last_all = pltpu.make_async_remote_copy(
        src_ref=w_ring.at[pl.ds(0, CTX - 1)],
        dst_ref=w_ring.at[pl.ds(0, CTX - 1)],
        send_sem=last_send,
        recv_sem=last_recv,
        device_id=(doc, lax.rem(pos + 1, CTX)),
        device_id_type=MESH,
    )
    deliver(5, grad_value)

    @pl.when(owns_piece)
    def _():
        own_all(7).wait_recv()

    @pl.when(jnp.logical_not(owns_piece))
    def _():
        own_all(8).wait_recv()

    f_turned[...] = f_recv[...].astype(F32).reshape(ROWS, 128).T
    for which in range(2):
        first = pl.multiple_of(64 * which + 16 * lax.rem(doc, 4), 16)
        filter_grad[which] = f_turned[pl.ds(first, 16), :]

    last_all.wait_recv()
    total = jnp.sum(w_ring[...].astype(F32), axis=0) * scale
    weight_grad[...] = jnp.where(odd, turn(total), total)[:, :64]

    for slot in range(6):
        ring_all(slot).wait_send()
    f_pair_copy.wait_send()
    w_pair_copy.wait_send()
    plane_all(0, f_sum, f_plane).wait_send()
    plane_all(1, w_sum, w_plane).wait_send()
    last_all.wait_send()

    @pl.when(owns_piece)
    def _():
        own_all(7).wait_send()

    @pl.when(jnp.logical_not(owns_piece))
    def _():
        own_all(8).wait_send()


def finish(*refs):
    sems = refs[12]
    copies = [pltpu.make_async_copy(refs[i], refs[6 + i], sems.at[i]) for i in range(6)]
    for copy in copies:
        copy.start()
    for copy in copies:
        copy.wait()


def on_device(value, gate_one, gate_two, filters, out_weight, grad_out):
    vmem = pl.BlockSpec(memory_space=pltpu.VMEM)
    anywhere = pl.BlockSpec(memory_space=pl.ANY)
    stream = pltpu.VMEM((ROWS, WIDTH), BF16)
    table = pltpu.VMEM((2 * BINS, 256), BF16)
    spectrum = pltpu.VMEM((2 * BINS, 256), F32)
    dma = pltpu.SemaphoreType.DMA
    shapes = [((ROWS, WIDTH), BF16)] * 4 + [((2, 16, ROWS), F32), ((16, 64), F32)]
    outs = pl.pallas_call(
        kernel,
        out_shape=tuple(pltpu.VMEM(*shape) for shape in shapes),
        in_specs=[anywhere] * 9,
        out_specs=[vmem] * 6,
        scratch_shapes=[
            stream, stream, stream, stream,
            pltpu.VMEM((WIDTH, WIDTH), BF16),
            table, table,
            pltpu.VMEM((BLK, 2 * BINS), BF16),
            pltpu.VMEM((2, 1024, 128), BF16),
            pltpu.VMEM((6, CTX, 64, 128), BF16),
            pltpu.VMEM((6, CTX, 64, 128), BF16),
            spectrum, spectrum, spectrum, spectrum, spectrum, spectrum,
            pltpu.VMEM((2, 2 * BINS, 256), BF16),
            pltpu.VMEM((BLK, 256), F32),
            pltpu.VMEM((ROWS, WIDTH), F32),
            pltpu.VMEM((BLK, 256), BF16),
            pltpu.VMEM((2, CHIPS, 16, WIDTH), BF16),
            pltpu.VMEM((CHIPS, 16, WIDTH), BF16),
            pltpu.VMEM((CHIPS, 16, WIDTH), BF16),
            pltpu.VMEM((CHIPS, 16, WIDTH), BF16),
            pltpu.VMEM((4, 16, 128), BF16),
            pltpu.VMEM((CTX, 16, 128), BF16),
            pltpu.VMEM((2, CHIPS, 32, 128), BF16),
            pltpu.VMEM((CHIPS, 32, 128), BF16),
            pltpu.VMEM((CHIPS, 32, 128), BF16),
            pltpu.VMEM((CHIPS, 32, 128), BF16),
            pltpu.VMEM((2, 16, 128), BF16),
            pltpu.VMEM((8, 16, 128), BF16),
            pltpu.VMEM((128, ROWS), F32),
            dma((9,)),
            dma((6,)),
            dma((6,)),
            dma((2,)),
            dma((2,)),
            dma((2,)),
            dma((2,)),
            dma,
            dma,
            dma,
            dma,
        ],
        compiler_params=pltpu.CompilerParams(collective_id=0, has_side_effects=True),
    )(
        value[0], gate_one[0], gate_two[0], grad_out[0], filters, out_weight,
        *(jnp.asarray(table) for table in tables()),
    )
    outs = pl.pallas_call(
        finish,
        out_shape=tuple(jax.ShapeDtypeStruct(*shape) for shape in shapes),
        in_specs=[vmem] * 6,
        out_specs=[anywhere] * 6,
        scratch_shapes=[dma((6,))],
        compiler_params=pltpu.CompilerParams(vmem_limit_bytes=1 << 20),
    )(*outs)
    mixed, grad_value, grad_gate_one, grad_gate_two, filter_grad, weight_grad = outs
    return (
        mixed[None], grad_value[None], grad_gate_one[None], grad_gate_two[None],
        jnp.swapaxes(filter_grad, 1, 2), weight_grad,
    )


def solution(mesh):
    stream = P("dp", "ctx", None)
    return jax.shard_map(
        on_device,
        mesh=mesh,
        in_specs=(stream, stream, stream, P(), P(), stream),
        out_specs=(stream, stream, stream, stream, P(None, "ctx", "dp"), P("dp", "ctx")),
        check_vma=False,
    )
```

```python
import numpy as np

import jax
import jax.numpy as jnp
from jax import lax
from jax.experimental import pallas as pl
from jax.experimental.pallas import tpu as pltpu
from jax.sharding import PartitionSpec as P

F32 = jnp.float32
BF16 = jnp.bfloat16
MESH = pl.DeviceIdType.MESH

CTX = 8
CHIPS = 16
WIDTH = 512
ROWS = 128
BLK = 256
BINS = 256
CHUNK = 16
UNROLL = 8
PLANE = sorted(
    ((dy, dx) for dy in range(4) for dx in range(4) if dy or dx),
    key=lambda d: -sum(min(step, 4 - step) for step in d),
)


def tables():
    bins = np.concatenate([np.arange(0, BINS, 2), np.arange(1, BINS, 2)])
    angle = 2.0 * np.pi * (bins[:, None] + 0.5) * np.arange(BLK)[None, :] / (2 * BLK)
    forward = np.concatenate([np.cos(angle), -np.sin(angle)], axis=0)
    inverse = forward.T / BINS

    def split(table):
        high = table.astype(BF16)
        low = (table - high.astype(np.float64)).astype(BF16)
        return high, low

    return split(forward) + split(inverse)[:1]


def lanes_low(rows):
    return lax.broadcasted_iota(jnp.int32, (rows, 128), 1) < 64


def turn(x, shift=64):
    return pltpu.roll(x, shift, 1)


def mix(a, b):
    low = lanes_low(a.shape[0])
    return jnp.where(low, a, turn(b)), jnp.where(low, turn(a), b)


def kernel(
    value_hbm, gate_one_hbm, gate_two_hbm, grad_out_hbm, filters_hbm, weight_hbm, fh_hbm, fl_hbm, ih_hbm,
    mixed, grad_value, grad_gate_one, grad_gate_two, filter_grad, weight_grad,
    value, gate_one, gate_two, grad_out, weight, fh, fl, ih, filt,
    sbuf, rbuf, g_first, g_second, v_spec, m_spec, s_spec, f_spec, product,
    first_conv, grad_gated, xt,
    w_part, w_pair, w_sum, w_plane, w_tiles, w_ring,
    f_part, f_pair, f_sum, f_plane, f_send, f_recv, f_turned,
    in_sem, z_send, z_recv, pair_send, pair_recv, plane_send, plane_recv,
    last_send, last_recv, own_send, own_recv,
):
    doc = lax.axis_index("dp")
    pos = lax.axis_index("ctx")
    core = lax.rem(doc, 2)
    chip = lax.div(doc, 2)

    barrier = pltpu.get_barrier_semaphore()
    for o in range(1, CTX):
        pl.semaphore_signal(barrier, inc=1, device_id=(doc, lax.rem(pos + o, CTX)), device_id_type=MESH)
    pl.semaphore_signal(barrier, inc=1, device_id=(2 * chip + 1 - core, pos), device_id_type=MESH)
    for o in range(1, CHIPS):
        peer = 2 * lax.rem(chip + o, CHIPS) + core
        pl.semaphore_signal(barrier, inc=1, device_id=(peer, pos), device_id_type=MESH)

    column = pl.multiple_of(lax.div(pos, 2) * 128, 128)
    loads = {}
    for i, (name, src, dst) in enumerate((
        ("value", value_hbm, value),
        ("filt", filters_hbm.at[:, :, pl.ds(column, 128)], filt),
        ("fh", fh_hbm, fh),
        ("fl", fl_hbm, fl),
        ("gate_one", gate_one_hbm, gate_one),
        ("grad_out", grad_out_hbm, grad_out),
        ("weight", weight_hbm, weight),
        ("gate_two", gate_two_hbm, gate_two),
        ("ih", ih_hbm, ih),
    )):
        loads[name] = pltpu.make_async_copy(src, dst, in_sem.at[i])
        loads[name].start()

    def pack_rows(slot, tile_of):
        for p in range(4):
            first, second = mix(tile_of(0, p), tile_of(1, p))
            sbuf[slot, 2 * p] = first.astype(BF16)
            sbuf[slot, 2 * p + 1] = second.astype(BF16)
        rbuf[slot, pos] = sbuf[slot, pos]

    def pack_blocks(slot, tiles):
        for t in range(2):
            for h in range(2):
                part = tiles[t][128 * h : 128 * h + 128]
                first, second = mix(part[:64], part[64:])
                sbuf[slot, 4 * t + h] = first.astype(BF16)
                sbuf[slot, 4 * t + 2 + h] = second.astype(BF16)
        rbuf[slot, pos] = sbuf[slot, pos]

    def ring_copy(slot, to, at):
        return pltpu.make_async_remote_copy(
            src_ref=sbuf.at[slot, to],
            dst_ref=rbuf.at[slot, at],
            send_sem=z_send.at[slot],
            recv_sem=z_recv.at[slot],
            device_id=(doc, to),
            device_id_type=MESH,
        )

    def ring_start(slot):
        for o in (4, 3, 5, 2, 6, 1, 7):
            ring_copy(slot, lax.rem(pos + o, CTX), pos).start()

    def ring_all(slot):
        most = pl.ds(0, CTX - 1)
        return pltpu.make_async_remote_copy(
            src_ref=sbuf.at[slot, most],
            dst_ref=rbuf.at[slot, most],
            send_sem=z_send.at[slot],
            recv_sem=z_recv.at[slot],
            device_id=(doc, lax.rem(pos + 1, CTX)),
            device_id_type=MESH,
        )

    def ring_wait(slot):
        ring_all(slot).wait_recv()

    def rows_tile(ref):
        return lambda h, p: ref[64 * h : 64 * h + 64, 128 * p : 128 * p + 128].astype(F32)

    loads["value"].wait()
    pack_rows(0, rows_tile(value))
    pl.semaphore_wait(barrier, CTX + CHIPS - 1)
    ring_start(0)

    def forward(spec):
        block = xt[...]
        spec[...] = jnp.dot(fh[...], block, preferred_element_type=F32) + jnp.dot(
            fl[...], block, preferred_element_type=F32
        )

    def inverse(slot=0):
        return jnp.dot(ih[...], product[slot], preferred_element_type=F32)

    def load(spec, r):
        a = spec[pl.ds(r, CHUNK), :]
        b = spec[pl.ds(BINS + r, CHUNK), :]
        return (a[:, :128], b[:, :128]), (a[:, 128:], b[:, 128:])

    def store(slot, r, low_blocks, high_blocks):
        for part in range(2):
            for t, block in enumerate((low_blocks, high_blocks)):
                product[slot, pl.ds(part * BINS + r, CHUNK), 128 * t : 128 * t + 128] = block[part].astype(BF16)

    def both(x):
        return tuple(turn(part) for part in x)

    def pick(a, b):
        low = lanes_low(CHUNK)
        return tuple(jnp.where(low, x, y) for x, y in zip(a, b))

    def low_only(x):
        return pick(x, (jnp.zeros_like(x[0]),) * 2)

    def high_only(x):
        return pick((jnp.zeros_like(x[0]),) * 2, x)

    def times(a, b):
        return a[0] * b[0] - a[1] * b[1], a[0] * b[1] + a[1] * b[0]

    def conj_times(a, b):
        return a[0] * b[0] + a[1] * b[1], a[0] * b[1] - a[1] * b[0]

    def plus(*terms):
        return sum(t[0] for t in terms[1:]) + terms[0][0], sum(t[1] for t in terms[1:]) + terms[0][1]

    def chunks(body, unroll=UNROLL):
        for half, sign in ((0, 1.0), (1, -1.0)):

            def step(i, carry):
                body(pl.multiple_of(half * (BINS // 2) + i * CHUNK, CHUNK), sign)
                return carry

            lax.fori_loop(0, BINS // 2 // CHUNK, step, 0, unroll=unroll)

    def spread(g01, g23):
        t01, t23 = both(g01), both(g23)
        return pick(g01, t01), pick(t01, g01), pick(g23, t23), t01, t23

    def convolve(filter_spec, data_spec):
        def body(r, sign):
            g01, g23 = load(filter_spec, r)
            x01, x23 = load(data_spec, r)
            h0, h1, h2, _, _ = spread(g01, g23)
            x10, x32 = both(x01), both(x23)
            x12 = pick(x10, x32)
            out01 = plus(times(h0, x01), times(high_only(g01), x10))
            out23 = plus(times(h0, x23), times(h1, x12), times(h2, x01), times(high_only(g23), x10))
            store(0, r, out01, out23)

        chunks(body)

    def correlate(filter_spec, data_spec, windows, slot=0):
        def body(r, sign):
            g01, g23 = load(filter_spec, r)
            y01, y23 = load(data_spec, r)
            if windows:
                t01, t23 = both(y01), both(y23)
                n01, n23 = pick(t01, t23), low_only(t23)
                y01 = (y01[0] + sign * n01[1], y01[1] - sign * n01[0])
                y23 = (y23[0] + sign * n23[1], y23[1] - sign * n23[0])
            h0, h1, h2, t01, t23 = spread(g01, g23)
            y10, y32 = both(y01), both(y23)
            y12 = pick(y10, y32)
            out01 = plus(
                conj_times(h0, y01), conj_times(h1, y12), conj_times(h2, y23), conj_times(low_only(t23), y32)
            )
            out23 = plus(conj_times(h0, y23), conj_times(low_only(t01), y32))
            store(slot, r, out01, out23)

        chunks(body, UNROLL // 2 if windows else UNROLL)

    odd = lax.rem(pos, 2) == 1

    def filter_windows(which, spec):
        for t in range(2):
            lag_tiles = []
            for k in (2 * t, 2 * t + 1):
                tile = filt[which, BLK * k : BLK * k + BLK, :].astype(F32)
                lag_tiles.append(jnp.where(odd, turn(tile), tile))
            xt[:, 128 * t : 128 * t + 128] = mix(*lag_tiles)[0].astype(BF16)
        forward(spec)

        def window(r, sign):
            h01, h23 = load(spec, r)
            t01, t23 = both(h01), both(h23)
            b01, b23 = high_only(t01), pick(t01, t23)
            for t, (h, b) in enumerate(((h01, b01), (h23, b23))):
                spec[pl.ds(r, CHUNK), 128 * t : 128 * t + 128] = h[0] - sign * b[1]
                spec[pl.ds(BINS + r, CHUNK), 128 * t : 128 * t + 128] = h[1] + sign * b[0]

        chunks(window)

    for name in ("filt", "fh", "fl", "gate_one"):
        loads[name].wait()
    pack_rows(1, rows_tile(gate_one))
    filter_windows(0, g_first)
    ring_start(1)
    for name in ("grad_out", "weight", "gate_two", "ih"):
        loads[name].wait()
    grad_gated[...] = lax.dot_general(
        grad_out[...], weight[...], (((1,), (1,)), ((), ())), preferred_element_type=F32
    )
    pack_rows(
        2,
        lambda h, p: (
            grad_gated[64 * h : 64 * h + 64, 128 * p : 128 * p + 128]
            * gate_two[64 * h : 64 * h + 64, 128 * p : 128 * p + 128].astype(F32)
        ).astype(BF16).astype(F32),
    )
    ring_start(2)
    filter_windows(1, g_second)

    def arrived(slot, t, h):
        return mix(rbuf[slot, 4 * t + h].astype(F32), rbuf[slot, 4 * t + 2 + h].astype(F32))

    def to_columns(slot, scale=None):
        for t in range(2):
            for h in range(2):
                for half, part in enumerate(arrived(slot, t, h)):
                    where = (
                        slice(128 * h + 64 * half, 128 * h + 64 * half + 64),
                        slice(128 * t, 128 * t + 128),
                    )
                    if scale is not None:
                        part = part * scale[where]
                    xt[where] = part.astype(BF16)

    def split_tiles(x):
        return x[:, :128], x[:, 128:]

    ring_wait(0)
    to_columns(0)
    forward(v_spec)
    convolve(g_first, v_spec)
    first_conv[...] = inverse()
    ring_wait(1)
    to_columns(1, first_conv)
    forward(m_spec)
    convolve(g_second, m_spec)
    pack_blocks(3, split_tiles(inverse()))
    ring_start(3)

    ring_wait(2)
    to_columns(2)
    forward(s_spec)
    correlate(g_second, s_spec, False)
    grad_mixed = inverse()
    pack_blocks(4, split_tiles(grad_mixed * first_conv[...]))
    to_columns(1, grad_mixed)
    forward(f_spec)

    def pair_copy(index, src, dst):
        return pltpu.make_async_remote_copy(
            src_ref=src.at[1 - core],
            dst_ref=dst,
            send_sem=pair_send.at[index],
            recv_sem=pair_recv.at[index],
            device_id=(2 * chip + 1 - core, pos),
            device_id_type=MESH,
        )

    row, col = lax.div(chip, 4), lax.rem(chip, 4)

    def piece_of(y, x):
        dy = lax.rem(y + 4 - lax.div(pos, 2), 4)
        dx = lax.rem(x + 4 - 2 * lax.rem(pos, 2), 4)
        away = jnp.where(dx >= 2, lax.rem(10 - dy, 8), 3 + lax.rem(dy + 1, 4))
        return 2 * lax.rem(pos + away, CTX) + lax.rem(dx, 2)

    def plane_start(index, src, dst, slot_of):
        for dy, dx in PLANE:
            y, x = lax.rem(row + dy, 4), lax.rem(col + dx, 4)
            pltpu.make_async_remote_copy(
                src_ref=src.at[slot_of(y, x)],
                dst_ref=dst.at[chip],
                send_sem=plane_send.at[index],
                recv_sem=plane_recv.at[index],
                device_id=(2 * (4 * y + x) + core, pos),
                device_id_type=MESH,
            ).start()
        dst[chip] = src[slot_of(row, col)]

    def plane_all(index, src, dst):
        most = pl.ds(0, CHIPS - 1)
        return pltpu.make_async_remote_copy(
            src_ref=src.at[most],
            dst_ref=dst.at[most],
            send_sem=plane_send.at[index],
            recv_sem=plane_recv.at[index],
            device_id=(2 * lax.rem(chip + 1, CHIPS) + core, pos),
            device_id_type=MESH,
        )

    correlate(v_spec, f_spec, True, 0)
    correlate(m_spec, s_spec, True, 1)
    lags = [inverse(which) for which in range(2)]
    for h in range(2):
        for t in range(2):
            where = (slice(128 * h, 128 * h + 128), slice(128 * t, 128 * t + 128))
            for k, part in enumerate(mix(lags[0][where], lags[1][where])):
                part = part.astype(BF16)
                for rho in range(4):
                    piece = 2 * (2 * (2 * t + k) + h) + rho // 2
                    f_part[rho % 2, piece] = part[32 * rho : 32 * rho + 32]
    f_pair_copy = pair_copy(0, f_part, f_pair)
    f_pair_copy.start()
    ring_start(4)
    def row_tile(slot, p):
        return mix(rbuf[slot, 2 * p].astype(F32), rbuf[slot, 2 * p + 1].astype(F32))

    ring_wait(3)
    for p in range(4):
        for half, part in enumerate(row_tile(3, p)):
            where = (slice(64 * half, 64 * half + 64), slice(128 * p, 128 * p + 128))
            grad_gate_two[where] = (grad_gated[where] * part).astype(BF16)
            grad_gated[where] = (gate_two[where].astype(F32) * part).astype(BF16).astype(F32)
    gated = grad_gated[...].astype(BF16)
    gated_t = grad_gated[...].T.astype(BF16)
    for c in range(4):
        part = jnp.dot(
            gated_t[128 * c : 128 * c + 128], grad_out[...], preferred_element_type=F32
        ).astype(BF16)
        for i in range(8):
            w_part[i % 2, 4 * c + i // 2] = part[16 * i : 16 * i + 16]
    w_pair_copy = pair_copy(1, w_part, w_pair)
    w_pair_copy.start()
    correlate(g_first, f_spec, False)
    pack_blocks(5, split_tiles(inverse()))
    ring_start(5)
    f_pair_copy.wait_recv()
    f_sum[...] = (f_part[core].astype(F32) + f_pair[...].astype(F32)).astype(BF16)
    plane_start(0, f_sum, f_plane, piece_of)

    w_pair_copy.wait_recv()
    w_sum[...] = (w_part[core].astype(F32) + w_pair[...].astype(F32)).astype(BF16)
    plane_start(1, w_sum, w_plane, lambda y, x: 4 * y + x)

    def deliver(slot, out):
        ring_wait(slot)
        for p in range(4):
            for half, part in enumerate(row_tile(slot, p)):
                out[64 * half : 64 * half + 64, 128 * p : 128 * p + 128] = part.astype(BF16)

    scale = 1.0 / 32

    plane_all(0, f_sum, f_plane).wait_recv()
    total = jnp.sum(f_plane[...].astype(F32), axis=0) * scale
    even = lax.rem(lax.div(lax.broadcasted_iota(jnp.int32, (16, 128), 1), 32), 2) == 0
    f_send[0] = jnp.where(even, total[:16], turn(total[16:], 32)).astype(BF16)
    f_send[1] = jnp.where(even, turn(total[:16], 96), total[16:]).astype(BF16)
    piece = piece_of(row, col)
    rho = 2 * lax.rem(piece, 2) + core
    for q in range(4):
        pltpu.make_async_remote_copy(
            src_ref=f_send.at[q // 2],
            dst_ref=f_recv.at[rho],
            send_sem=own_send,
            recv_sem=own_recv,
            device_id=(4 * pos + q, lax.div(piece, 2)),
            device_id_type=MESH,
        ).start()
    own_all = pltpu.make_async_remote_copy(
        src_ref=f_recv,
        dst_ref=f_recv,
        send_sem=own_send,
        recv_sem=own_recv,
        device_id=(doc, lax.rem(pos + 1, CTX)),
        device_id_type=MESH,
    )

    plane_all(1, w_sum, w_plane).wait_recv()
    w_total = jnp.sum(w_plane[...].astype(F32), axis=0).astype(BF16)
    for p in range(4):
        w_tiles[p] = w_total[:, 128 * p : 128 * p + 128]
    for o in (4, 3, 5, 2, 6, 1, 7):
        to = lax.rem(pos + o, CTX)
        pltpu.make_async_remote_copy(
            src_ref=w_tiles.at[lax.div(to, 2)],
            dst_ref=w_ring.at[pos],
            send_sem=last_send,
            recv_sem=last_recv,
            device_id=(doc, to),
            device_id_type=MESH,
        ).start()
    w_ring[pos] = w_tiles[lax.div(pos, 2)]
    last_all = pltpu.make_async_remote_copy(
        src_ref=w_ring.at[pl.ds(0, CTX - 1)],
        dst_ref=w_ring.at[pl.ds(0, CTX - 1)],
        send_sem=last_send,
        recv_sem=last_recv,
        device_id=(doc, lax.rem(pos + 1, CTX)),
        device_id_type=MESH,
    )
    deliver(4, grad_gate_one)
    deliver(5, grad_value)
    mixed[...] = jnp.dot(gated, weight[...], preferred_element_type=F32).astype(BF16)

    own_all.wait_recv()
    lags = []
    for rho in range(4):
        part = f_recv[rho].astype(F32)
        lags += [part, turn(part, 96)]
    f_turned[...] = jnp.concatenate(lags, axis=0).T
    for which in range(2):
        first = pl.multiple_of(64 * which + 16 * core, 16)
        filter_grad[which] = f_turned[pl.ds(first, 16), :]

    last_all.wait_recv()
    total = jnp.sum(w_ring[...].astype(F32), axis=0) * scale
    weight_grad[...] = jnp.where(odd, turn(total), total)[:, :64]

    for slot in range(6):
        ring_all(slot).wait_send()
    f_pair_copy.wait_send()
    w_pair_copy.wait_send()
    plane_all(0, f_sum, f_plane).wait_send()
    plane_all(1, w_sum, w_plane).wait_send()
    last_all.wait_send()

    own_all.wait_send()


def finish(*refs):
    sems = refs[12]
    copies = [pltpu.make_async_copy(refs[i], refs[6 + i], sems.at[i]) for i in range(6)]
    for copy in copies:
        copy.start()
    for copy in copies:
        copy.wait()


def on_device(value, gate_one, gate_two, filters, out_weight, grad_out):
    vmem = pl.BlockSpec(memory_space=pltpu.VMEM)
    anywhere = pl.BlockSpec(memory_space=pl.ANY)
    stream = pltpu.VMEM((ROWS, WIDTH), BF16)
    table = pltpu.VMEM((2 * BINS, 256), BF16)
    spectrum = pltpu.VMEM((2 * BINS, 256), F32)
    dma = pltpu.SemaphoreType.DMA
    shapes = [((ROWS, WIDTH), BF16)] * 4 + [((2, 16, ROWS), F32), ((16, 64), F32)]
    outs = pl.pallas_call(
        kernel,
        out_shape=tuple(pltpu.VMEM(*shape) for shape in shapes),
        in_specs=[anywhere] * 9,
        out_specs=[vmem] * 6,
        scratch_shapes=[
            stream, stream, stream, stream,
            pltpu.VMEM((WIDTH, WIDTH), BF16),
            table, table,
            pltpu.VMEM((BLK, 2 * BINS), BF16),
            pltpu.VMEM((2, 1024, 128), BF16),
            pltpu.VMEM((6, CTX, 64, 128), BF16),
            pltpu.VMEM((6, CTX, 64, 128), BF16),
            spectrum, spectrum, spectrum, spectrum, spectrum, spectrum,
            pltpu.VMEM((2, 2 * BINS, 256), BF16),
            pltpu.VMEM((BLK, 256), F32),
            pltpu.VMEM((ROWS, WIDTH), F32),
            pltpu.VMEM((BLK, 256), BF16),
            pltpu.VMEM((2, CHIPS, 16, WIDTH), BF16),
            pltpu.VMEM((CHIPS, 16, WIDTH), BF16),
            pltpu.VMEM((CHIPS, 16, WIDTH), BF16),
            pltpu.VMEM((CHIPS, 16, WIDTH), BF16),
            pltpu.VMEM((4, 16, 128), BF16),
            pltpu.VMEM((CTX, 16, 128), BF16),
            pltpu.VMEM((2, CHIPS, 32, 128), BF16),
            pltpu.VMEM((CHIPS, 32, 128), BF16),
            pltpu.VMEM((CHIPS, 32, 128), BF16),
            pltpu.VMEM((CHIPS, 32, 128), BF16),
            pltpu.VMEM((2, 16, 128), BF16),
            pltpu.VMEM((4, 16, 128), BF16),
            pltpu.VMEM((128, ROWS), F32),
            dma((9,)),
            dma((6,)),
            dma((6,)),
            dma((2,)),
            dma((2,)),
            dma((2,)),
            dma((2,)),
            dma,
            dma,
            dma,
            dma,
        ],
        compiler_params=pltpu.CompilerParams(collective_id=0, has_side_effects=True),
    )(
        value[0], gate_one[0], gate_two[0], grad_out[0], filters, out_weight,
        *(jnp.asarray(table) for table in tables()),
    )
    outs = pl.pallas_call(
        finish,
        out_shape=tuple(jax.ShapeDtypeStruct(*shape) for shape in shapes),
        in_specs=[vmem] * 6,
        out_specs=[anywhere] * 6,
        scratch_shapes=[dma((6,))],
        compiler_params=pltpu.CompilerParams(vmem_limit_bytes=1 << 20),
    )(*outs)
    mixed, grad_value, grad_gate_one, grad_gate_two, filter_grad, weight_grad = outs
    return (
        mixed[None], grad_value[None], grad_gate_one[None], grad_gate_two[None],
        jnp.swapaxes(filter_grad, 1, 2), weight_grad,
    )


def solution(mesh):
    stream = P("dp", "ctx", None)
    return jax.shard_map(
        on_device,
        mesh=mesh,
        in_specs=(stream, stream, stream, P(), P(), stream),
        out_specs=(stream, stream, stream, stream, P(None, "ctx", "dp"), P("dp", "ctx")),
        check_vma=False,
    )
```

```python
import numpy as np

import jax
import jax.numpy as jnp
from jax import lax
from jax.experimental import pallas as pl
from jax.experimental.pallas import tpu as pltpu
from jax.sharding import PartitionSpec as P

F32 = jnp.float32
BF16 = jnp.bfloat16
MESH = pl.DeviceIdType.MESH

CTX = 8
CHIPS = 16
WIDTH = 512
ROWS = 128
BLK = 256
BINS = 256
CHUNK = 16
UNROLL = 8
PLANE = sorted(
    ((dy, dx) for dy in range(4) for dx in range(4) if dy or dx),
    key=lambda d: -sum(min(step, 4 - step) for step in d),
)


def tables():
    bins = np.concatenate([np.arange(0, BINS, 2), np.arange(1, BINS, 2)])
    angle = 2.0 * np.pi * (bins[:, None] + 0.5) * np.arange(BLK)[None, :] / (2 * BLK)
    forward = np.concatenate([np.cos(angle), -np.sin(angle)], axis=0)
    inverse = forward.T / BINS

    def split(table):
        high = table.astype(BF16)
        low = (table - high.astype(np.float64)).astype(BF16)
        return high, low

    return split(forward) + split(inverse)[:1]


def lanes_low(rows):
    return lax.broadcasted_iota(jnp.int32, (rows, 128), 1) < 64


def turn(x, shift=64):
    return pltpu.roll(x, shift, 1)


def mix(a, b):
    low = lanes_low(a.shape[0])
    return jnp.where(low, a, turn(b)), jnp.where(low, turn(a), b)


def kernel(
    value_hbm, gate_one_hbm, gate_two_hbm, grad_out_hbm, filters_hbm, weight_hbm, fh_hbm, fl_hbm, ih_hbm,
    mixed, grad_value, grad_gate_one, grad_gate_two, filter_grad, weight_grad,
    value, gate_one, gate_two, grad_out, weight, fh, fl, ih, filt,
    sbuf, rbuf, g_first, g_second, v_spec, m_spec, s_spec, f_spec, forms, product,
    first_conv, grad_gated, xt,
    w_part, w_pair, w_sum, w_plane, w_tiles, w_ring,
    f_part, f_pair, f_sum, f_plane, f_send, f_recv, f_turned,
    in_sem, z_send, z_recv, pair_send, pair_recv, plane_send, plane_recv,
    last_send, last_recv, own_send, own_recv,
):
    doc = lax.axis_index("dp")
    pos = lax.axis_index("ctx")
    core = lax.rem(doc, 2)
    chip = lax.div(doc, 2)

    barrier = pltpu.get_barrier_semaphore()
    row, col = lax.div(chip, 4), lax.rem(chip, 4)
    for o in (4, 3, 5, 2, 6, 1, 7):
        pl.semaphore_signal(barrier, inc=1, device_id=(doc, lax.rem(pos + o, CTX)), device_id_type=MESH)
    for dy, dx in PLANE:
        peer = 2 * (4 * lax.rem(row + dy, 4) + lax.rem(col + dx, 4)) + core
        pl.semaphore_signal(barrier, inc=1, device_id=(peer, pos), device_id_type=MESH)
    pl.semaphore_signal(barrier, inc=1, device_id=(2 * chip + 1 - core, pos), device_id_type=MESH)

    column = pl.multiple_of(lax.div(pos, 2) * 128, 128)
    loads = {}
    for i, (name, src, dst) in enumerate((
        ("value", value_hbm, value),
        ("filt", filters_hbm.at[:, :, pl.ds(column, 128)], filt),
        ("fh", fh_hbm, fh),
        ("fl", fl_hbm, fl),
        ("gate_one", gate_one_hbm, gate_one),
        ("grad_out", grad_out_hbm, grad_out),
        ("weight", weight_hbm, weight),
        ("gate_two", gate_two_hbm, gate_two),
        ("ih", ih_hbm, ih),
    )):
        loads[name] = pltpu.make_async_copy(src, dst, in_sem.at[i])
        loads[name].start()

    def pack_rows(slot, tile_of):
        for p in range(4):
            first, second = mix(tile_of(0, p), tile_of(1, p))
            sbuf[slot, 2 * p] = first.astype(BF16)
            sbuf[slot, 2 * p + 1] = second.astype(BF16)
        rbuf[slot, pos] = sbuf[slot, pos]

    def pack_blocks(slot, tiles):
        for t in range(2):
            for h in range(2):
                part = tiles[t][128 * h : 128 * h + 128]
                first, second = mix(part[:64], part[64:])
                sbuf[slot, 4 * t + h] = first.astype(BF16)
                sbuf[slot, 4 * t + 2 + h] = second.astype(BF16)
        rbuf[slot, pos] = sbuf[slot, pos]

    def ring_copy(slot, to, at):
        return pltpu.make_async_remote_copy(
            src_ref=sbuf.at[slot, to],
            dst_ref=rbuf.at[slot, at],
            send_sem=z_send.at[slot],
            recv_sem=z_recv.at[slot],
            device_id=(doc, to),
            device_id_type=MESH,
        )

    def ring_start(slot):
        for o in (4, 3, 5, 2, 6, 1, 7):
            ring_copy(slot, lax.rem(pos + o, CTX), pos).start()

    def ring_all(slot):
        most = pl.ds(0, CTX - 1)
        return pltpu.make_async_remote_copy(
            src_ref=sbuf.at[slot, most],
            dst_ref=rbuf.at[slot, most],
            send_sem=z_send.at[slot],
            recv_sem=z_recv.at[slot],
            device_id=(doc, lax.rem(pos + 1, CTX)),
            device_id_type=MESH,
        )

    def ring_wait(slot):
        ring_all(slot).wait_recv()

    def rows_tile(ref):
        return lambda h, p: ref[64 * h : 64 * h + 64, 128 * p : 128 * p + 128].astype(F32)

    loads["value"].wait()
    pack_rows(0, rows_tile(value))
    pl.semaphore_wait(barrier, CTX + CHIPS - 1)
    ring_start(0)

    def forward(spec):
        block = xt[...]
        spec[...] = jnp.dot(fh[...], block, preferred_element_type=F32) + jnp.dot(
            fl[...], block, preferred_element_type=F32
        )

    def inverse(slot=0):
        return jnp.dot(ih[...], product[slot], preferred_element_type=F32)

    def load(spec, r):
        a = spec[pl.ds(r, CHUNK), :]
        b = spec[pl.ds(BINS + r, CHUNK), :]
        return (a[:, :128], b[:, :128]), (a[:, 128:], b[:, 128:])

    def store(slot, r, low_blocks, high_blocks):
        for part in range(2):
            for t, block in enumerate((low_blocks, high_blocks)):
                product[slot, pl.ds(part * BINS + r, CHUNK), 128 * t : 128 * t + 128] = block[part].astype(BF16)

    def both(x):
        return tuple(turn(part) for part in x)

    def pick(a, b):
        low = lanes_low(CHUNK)
        return tuple(jnp.where(low, x, y) for x, y in zip(a, b))

    def low_only(x):
        return pick(x, (jnp.zeros_like(x[0]),) * 2)

    def high_only(x):
        return pick((jnp.zeros_like(x[0]),) * 2, x)

    def times(a, b):
        return a[0] * b[0] - a[1] * b[1], a[0] * b[1] + a[1] * b[0]

    def conj_times(a, b):
        return a[0] * b[0] + a[1] * b[1], a[0] * b[1] - a[1] * b[0]

    def plus(*terms):
        return sum(t[0] for t in terms[1:]) + terms[0][0], sum(t[1] for t in terms[1:]) + terms[0][1]

    def chunks(body, unroll=UNROLL):
        for half, sign in ((0, 1.0), (1, -1.0)):

            def step(i, carry):
                body(pl.multiple_of(half * (BINS // 2) + i * CHUNK, CHUNK), sign)
                return carry

            lax.fori_loop(0, BINS // 2 // CHUNK, step, 0, unroll=unroll)

    def spread(g01, g23):
        t01, t23 = both(g01), both(g23)
        return pick(g01, t01), pick(t01, g01), pick(g23, t23), t01, t23

    def convolve(filter_spec, data_spec):
        def body(r, sign):
            g01, g23 = load(filter_spec, r)
            x01, x23 = load(data_spec, r)
            h0, h1, h2, _, _ = spread(g01, g23)
            x10, x32 = both(x01), both(x23)
            x12 = pick(x10, x32)
            out01 = plus(times(h0, x01), times(high_only(g01), x10))
            out23 = plus(times(h0, x23), times(h1, x12), times(h2, x01), times(high_only(g23), x10))
            store(0, r, out01, out23)

        chunks(body)

    def forms_of(spec):
        def at(r):
            h0, h1, h2, t01, t23 = spread(*load(spec, r))
            return h0, h1, h2, low_only(t23), low_only(t01)

        return at

    def prepare(index, spec):
        def body(r, sign):
            for n, form in enumerate(forms_of(spec)(r)):
                for part in range(2):
                    forms[index, n, pl.ds(part * BINS + r, CHUNK), :] = form[part]

        chunks(body)

        def at(r):
            return tuple(
                tuple(forms[index, n, pl.ds(part * BINS + r, CHUNK), :] for part in range(2)) for n in range(5)
            )

        return at

    def correlate(filter_forms, data_spec, windows, slot=0):
        def body(r, sign):
            y01, y23 = load(data_spec, r)
            if windows:
                t01, t23 = both(y01), both(y23)
                n01, n23 = pick(t01, t23), low_only(t23)
                y01 = (y01[0] + sign * n01[1], y01[1] - sign * n01[0])
                y23 = (y23[0] + sign * n23[1], y23[1] - sign * n23[0])
            h0, h1, h2, low3, low1 = filter_forms(r)
            y10, y32 = both(y01), both(y23)
            y12 = pick(y10, y32)
            out01 = plus(
                conj_times(h0, y01), conj_times(h1, y12), conj_times(h2, y23), conj_times(low3, y32)
            )
            out23 = plus(conj_times(h0, y23), conj_times(low1, y32))
            store(slot, r, out01, out23)

        chunks(body, UNROLL)

    odd = lax.rem(pos, 2) == 1

    def filter_windows(which, spec):
        for t in range(2):
            lag_tiles = []
            for k in (2 * t, 2 * t + 1):
                tile = filt[which, BLK * k : BLK * k + BLK, :].astype(F32)
                lag_tiles.append(jnp.where(odd, turn(tile), tile))
            xt[:, 128 * t : 128 * t + 128] = mix(*lag_tiles)[0].astype(BF16)
        forward(spec)

        def window(r, sign):
            h01, h23 = load(spec, r)
            t01, t23 = both(h01), both(h23)
            b01, b23 = high_only(t01), pick(t01, t23)
            for t, (h, b) in enumerate(((h01, b01), (h23, b23))):
                spec[pl.ds(r, CHUNK), 128 * t : 128 * t + 128] = h[0] - sign * b[1]
                spec[pl.ds(BINS + r, CHUNK), 128 * t : 128 * t + 128] = h[1] + sign * b[0]

        chunks(window)

    for name in ("filt", "fh", "fl", "gate_one"):
        loads[name].wait()
    pack_rows(1, rows_tile(gate_one))
    filter_windows(0, g_first)
    ring_start(1)
    for name in ("grad_out", "weight", "gate_two", "ih"):
        loads[name].wait()
    grad_gated[...] = lax.dot_general(
        grad_out[...], weight[...], (((1,), (1,)), ((), ())), preferred_element_type=F32
    )
    pack_rows(
        2,
        lambda h, p: (
            grad_gated[64 * h : 64 * h + 64, 128 * p : 128 * p + 128]
            * gate_two[64 * h : 64 * h + 64, 128 * p : 128 * p + 128].astype(F32)
        ).astype(BF16).astype(F32),
    )
    ring_start(2)
    filter_windows(1, g_second)

    def arrived(slot, t, h):
        return mix(rbuf[slot, 4 * t + h].astype(F32), rbuf[slot, 4 * t + 2 + h].astype(F32))

    def to_columns(slot, scale=None):
        for t in range(2):
            for h in range(2):
                for half, part in enumerate(arrived(slot, t, h)):
                    where = (
                        slice(128 * h + 64 * half, 128 * h + 64 * half + 64),
                        slice(128 * t, 128 * t + 128),
                    )
                    if scale is not None:
                        part = part * scale[where]
                    xt[where] = part.astype(BF16)

    def split_tiles(x):
        return x[:, :128], x[:, 128:]

    second_forms = prepare(0, g_second)
    ring_wait(0)
    to_columns(0)
    forward(v_spec)
    convolve(g_first, v_spec)
    first_conv[...] = inverse()
    value_forms = prepare(1, v_spec)
    ring_wait(1)
    to_columns(1, first_conv)
    forward(m_spec)
    convolve(g_second, m_spec)
    pack_blocks(3, split_tiles(inverse()))
    ring_start(3)

    mixed_forms = prepare(2, m_spec)
    ring_wait(2)
    to_columns(2)
    forward(s_spec)
    correlate(second_forms, s_spec, False)
    grad_mixed = inverse()
    to_columns(1, grad_mixed)
    forward(f_spec)

    def pair_copy(index, src, dst):
        return pltpu.make_async_remote_copy(
            src_ref=src.at[1 - core],
            dst_ref=dst,
            send_sem=pair_send.at[index],
            recv_sem=pair_recv.at[index],
            device_id=(2 * chip + 1 - core, pos),
            device_id_type=MESH,
        )

    def piece_of(y, x):
        dy = lax.rem(y + 4 - lax.div(pos, 2), 4)
        dx = lax.rem(x + 4 - 2 * lax.rem(pos, 2), 4)
        away = jnp.where(dx >= 2, lax.rem(10 - dy, 8), 3 + lax.rem(dy + 1, 4))
        return 2 * lax.rem(pos + away, CTX) + lax.rem(dx, 2)

    def plane_start(index, src, dst, slot_of):
        for dy, dx in PLANE:
            y, x = lax.rem(row + dy, 4), lax.rem(col + dx, 4)
            pltpu.make_async_remote_copy(
                src_ref=src.at[slot_of(y, x)],
                dst_ref=dst.at[chip],
                send_sem=plane_send.at[index],
                recv_sem=plane_recv.at[index],
                device_id=(2 * (4 * y + x) + core, pos),
                device_id_type=MESH,
            ).start()
        dst[chip] = src[slot_of(row, col)]

    def plane_all(index, src, dst):
        most = pl.ds(0, CHIPS - 1)
        return pltpu.make_async_remote_copy(
            src_ref=src.at[most],
            dst_ref=dst.at[most],
            send_sem=plane_send.at[index],
            recv_sem=plane_recv.at[index],
            device_id=(2 * lax.rem(chip + 1, CHIPS) + core, pos),
            device_id_type=MESH,
        )

    correlate(value_forms, f_spec, True, 0)
    correlate(mixed_forms, s_spec, True, 1)
    lags = [inverse(which) for which in range(2)]
    for h in range(2):
        for t in range(2):
            where = (slice(128 * h, 128 * h + 128), slice(128 * t, 128 * t + 128))
            for k, part in enumerate(mix(lags[0][where], lags[1][where])):
                part = part.astype(BF16)
                for rho in range(4):
                    piece = 2 * (2 * (2 * t + k) + h) + rho // 2
                    f_part[rho % 2, piece] = part[32 * rho : 32 * rho + 32]
    f_pair_copy = pair_copy(0, f_part, f_pair)
    f_pair_copy.start()
    pack_blocks(4, split_tiles(grad_mixed * first_conv[...]))
    ring_start(4)
    def row_tile(slot, p):
        return mix(rbuf[slot, 2 * p].astype(F32), rbuf[slot, 2 * p + 1].astype(F32))

    ring_wait(3)
    for p in range(4):
        for half, part in enumerate(row_tile(3, p)):
            where = (slice(64 * half, 64 * half + 64), slice(128 * p, 128 * p + 128))
            grad_gate_two[where] = (grad_gated[where] * part).astype(BF16)
            grad_gated[where] = (gate_two[where].astype(F32) * part).astype(BF16).astype(F32)
    gated = grad_gated[...].astype(BF16)
    gated_t = grad_gated[...].T.astype(BF16)
    for c in range(4):
        part = jnp.dot(
            gated_t[128 * c : 128 * c + 128], grad_out[...], preferred_element_type=F32
        ).astype(BF16)
        for i in range(8):
            w_part[i % 2, 4 * c + i // 2] = part[16 * i : 16 * i + 16]
    w_pair_copy = pair_copy(1, w_part, w_pair)
    w_pair_copy.start()
    f_pair_copy.wait_recv()
    f_sum[...] = (f_part[core].astype(F32) + f_pair[...].astype(F32)).astype(BF16)
    plane_start(0, f_sum, f_plane, piece_of)

    w_pair_copy.wait_recv()
    w_sum[...] = (w_part[core].astype(F32) + w_pair[...].astype(F32)).astype(BF16)
    plane_start(1, w_sum, w_plane, lambda y, x: 4 * y + x)

    correlate(forms_of(g_first), f_spec, False)
    pack_blocks(5, split_tiles(inverse()))
    ring_start(5)
    def deliver(slot, out):
        ring_wait(slot)
        for p in range(4):
            for half, part in enumerate(row_tile(slot, p)):
                out[64 * half : 64 * half + 64, 128 * p : 128 * p + 128] = part.astype(BF16)

    scale = 1.0 / 32

    plane_all(0, f_sum, f_plane).wait_recv()
    total = jnp.sum(f_plane[...].astype(F32), axis=0) * scale
    even = lax.rem(lax.div(lax.broadcasted_iota(jnp.int32, (16, 128), 1), 32), 2) == 0
    f_send[0] = jnp.where(even, total[:16], turn(total[16:], 32)).astype(BF16)
    f_send[1] = jnp.where(even, turn(total[:16], 96), total[16:]).astype(BF16)
    piece = piece_of(row, col)
    rho = 2 * lax.rem(piece, 2) + core
    for q in range(4):
        pltpu.make_async_remote_copy(
            src_ref=f_send.at[q // 2],
            dst_ref=f_recv.at[rho],
            send_sem=own_send,
            recv_sem=own_recv,
            device_id=(4 * pos + q, lax.div(piece, 2)),
            device_id_type=MESH,
        ).start()
    own_all = pltpu.make_async_remote_copy(
        src_ref=f_recv,
        dst_ref=f_recv,
        send_sem=own_send,
        recv_sem=own_recv,
        device_id=(doc, lax.rem(pos + 1, CTX)),
        device_id_type=MESH,
    )

    plane_all(1, w_sum, w_plane).wait_recv()
    w_total = jnp.sum(w_plane[...].astype(F32), axis=0).astype(BF16)
    for p in range(4):
        w_tiles[p] = w_total[:, 128 * p : 128 * p + 128]
    for o in (4, 3, 5, 2, 6, 1, 7):
        to = lax.rem(pos + o, CTX)
        pltpu.make_async_remote_copy(
            src_ref=w_tiles.at[lax.div(to, 2)],
            dst_ref=w_ring.at[pos],
            send_sem=last_send,
            recv_sem=last_recv,
            device_id=(doc, to),
            device_id_type=MESH,
        ).start()
    w_ring[pos] = w_tiles[lax.div(pos, 2)]
    last_all = pltpu.make_async_remote_copy(
        src_ref=w_ring.at[pl.ds(0, CTX - 1)],
        dst_ref=w_ring.at[pl.ds(0, CTX - 1)],
        send_sem=last_send,
        recv_sem=last_recv,
        device_id=(doc, lax.rem(pos + 1, CTX)),
        device_id_type=MESH,
    )
    deliver(4, grad_gate_one)
    deliver(5, grad_value)
    mixed[...] = jnp.dot(gated, weight[...], preferred_element_type=F32).astype(BF16)

    own_all.wait_recv()
    lags = []
    for rho in range(4):
        part = f_recv[rho].astype(F32)
        lags += [part, turn(part, 96)]
    f_turned[...] = jnp.concatenate(lags, axis=0).T
    for which in range(2):
        first = pl.multiple_of(64 * which + 16 * core, 16)
        filter_grad[which] = f_turned[pl.ds(first, 16), :]

    last_all.wait_recv()
    total = jnp.sum(w_ring[...].astype(F32), axis=0) * scale
    weight_grad[...] = jnp.where(odd, turn(total), total)[:, :64]

    for slot in range(6):
        ring_all(slot).wait_send()
    f_pair_copy.wait_send()
    w_pair_copy.wait_send()
    plane_all(0, f_sum, f_plane).wait_send()
    plane_all(1, w_sum, w_plane).wait_send()
    last_all.wait_send()

    own_all.wait_send()


def finish(*refs):
    sems = refs[12]
    copies = [pltpu.make_async_copy(refs[i], refs[6 + i], sems.at[i]) for i in range(6)]
    for copy in copies:
        copy.start()
    for copy in copies:
        copy.wait()


def on_device(value, gate_one, gate_two, filters, out_weight, grad_out):
    vmem = pl.BlockSpec(memory_space=pltpu.VMEM)
    anywhere = pl.BlockSpec(memory_space=pl.ANY)
    stream = pltpu.VMEM((ROWS, WIDTH), BF16)
    table = pltpu.VMEM((2 * BINS, 256), BF16)
    spectrum = pltpu.VMEM((2 * BINS, 256), F32)
    dma = pltpu.SemaphoreType.DMA
    shapes = [((ROWS, WIDTH), BF16)] * 4 + [((2, 16, ROWS), F32), ((16, 64), F32)]
    outs = pl.pallas_call(
        kernel,
        out_shape=tuple(pltpu.VMEM(*shape) for shape in shapes),
        in_specs=[anywhere] * 9,
        out_specs=[vmem] * 6,
        scratch_shapes=[
            stream, stream, stream, stream,
            pltpu.VMEM((WIDTH, WIDTH), BF16),
            table, table,
            pltpu.VMEM((BLK, 2 * BINS), BF16),
            pltpu.VMEM((2, 1024, 128), BF16),
            pltpu.VMEM((6, CTX, 64, 128), BF16),
            pltpu.VMEM((6, CTX, 64, 128), BF16),
            spectrum, spectrum, spectrum, spectrum, spectrum, spectrum,
            pltpu.VMEM((3, 5, 2 * BINS, 128), F32),
            pltpu.VMEM((2, 2 * BINS, 256), BF16),
            pltpu.VMEM((BLK, 256), F32),
            pltpu.VMEM((ROWS, WIDTH), F32),
            pltpu.VMEM((BLK, 256), BF16),
            pltpu.VMEM((2, CHIPS, 16, WIDTH), BF16),
            pltpu.VMEM((CHIPS, 16, WIDTH), BF16),
            pltpu.VMEM((CHIPS, 16, WIDTH), BF16),
            pltpu.VMEM((CHIPS, 16, WIDTH), BF16),
            pltpu.VMEM((4, 16, 128), BF16),
            pltpu.VMEM((CTX, 16, 128), BF16),
            pltpu.VMEM((2, CHIPS, 32, 128), BF16),
            pltpu.VMEM((CHIPS, 32, 128), BF16),
            pltpu.VMEM((CHIPS, 32, 128), BF16),
            pltpu.VMEM((CHIPS, 32, 128), BF16),
            pltpu.VMEM((2, 16, 128), BF16),
            pltpu.VMEM((4, 16, 128), BF16),
            pltpu.VMEM((128, ROWS), F32),
            dma((9,)),
            dma((6,)),
            dma((6,)),
            dma((2,)),
            dma((2,)),
            dma((2,)),
            dma((2,)),
            dma,
            dma,
            dma,
            dma,
        ],
        compiler_params=pltpu.CompilerParams(collective_id=0, has_side_effects=True),
    )(
        value[0], gate_one[0], gate_two[0], grad_out[0], filters, out_weight,
        *(jnp.asarray(table) for table in tables()),
    )
    outs = pl.pallas_call(
        finish,
        out_shape=tuple(jax.ShapeDtypeStruct(*shape) for shape in shapes),
        in_specs=[vmem] * 6,
        out_specs=[anywhere] * 6,
        scratch_shapes=[dma((6,))],
        compiler_params=pltpu.CompilerParams(vmem_limit_bytes=1 << 20),
    )(*outs)
    mixed, grad_value, grad_gate_one, grad_gate_two, filter_grad, weight_grad = outs
    return (
        mixed[None], grad_value[None], grad_gate_one[None], grad_gate_two[None],
        jnp.swapaxes(filter_grad, 1, 2), weight_grad,
    )


def solution(mesh):
    stream = P("dp", "ctx", None)
    return jax.shard_map(
        on_device,
        mesh=mesh,
        in_specs=(stream, stream, stream, P(), P(), stream),
        out_specs=(stream, stream, stream, stream, P(None, "ctx", "dp"), P("dp", "ctx")),
        check_vma=False,
    )
```
